512 devices in a mesh: cells: 128 (over y, z_hi, x, core), grp: 4 (over z_lo).
Axes of the slice: x: 4, y: 8, z: 8 (z_hi: 2, z_lo: 4; z = z_hi * 4 + z_lo), core: 2. Of those that a mesh axis runs over, the one named last changes fastest.
Arguments:
- fraction: float32 [3, 128, 4, 512], P(None, 'cells', 'grp'), may hold values from 0 to 1
- velocity: float32 [3, 128, 4, 512], P(None, 'cells', 'grp'), may hold values from -1.8 to 1.8
- anchor: int32 [3, 128, 4, 512], P(None, 'cells', 'grp'), may hold values from 0 to 254, as said below
- atom_types: int32 [128, 4, 512], P('cells', 'grp'), may hold values from 0 to 7
- counts: int32 [128, 4], P('cells', 'grp'), may hold values from 64 to 512, as said below
- type_table: float32 [3, 8], replicated, may hold values from 0.7 to 2.8, as said below
- target: float32 [512, 64, 256], P('cells', 'grp'), may hold values from -0.3 to 0.3
Outputs:
- final_velocity: float32 [3, 128, 4, 512], P(None, 'cells', 'grp')
- displacement: float32 [3, 128, 4, 512], P(None, 'cells', 'grp')
- potential: float32 [512, 64, 256], P('cells', 'grp')
The draws below stay inside these ranges and needn't reach their ends.
Inputs may be any that keep to these rules, and one draw needn't show every extreme that they name: `counts`: some cell holds exactly 512 live atoms in every draw; dead slots follow the live ones. `anchor`: component 0 is below 4, component 1 below 16, component 2 below 255. `type_table`: all entries are positive.
All inputs are finite; a program needn't handle non-finite values.
Results may differ from the reference program's by a relative error of at most 0.0003.
Values sent between devices are 32-bit elements; how exact they have to be, the bound alone decides.
No kernel may reach another device: no remote copies, remote signals or barrier semaphores. Data moves between devices by JAX's collectives and lax.ppermute only.
A program may use at most 64 MiB of HBM per device.

```python
import jax
import jax.numpy as jnp
from jax import lax

BX = 4
BYD = 16
GZ = 256
ATOM_DEV = 512
TYPES = 8
STEPS = 2
NX = 512
NY = 64
N_CELLS = 128
N_GRP = 4


def draw_counts(key, part):
    first_key, second_key = jax.random.split(jax.random.fold_in(key, 11))
    levels = jax.random.randint(first_key, (N_CELLS, N_GRP), 0, 4, dtype=jnp.int32)
    values = (ATOM_DEV // jnp.power(jnp.int32(2), levels)).astype(jnp.int32)
    chosen = jax.random.randint(second_key, (), 0, N_CELLS * N_GRP, dtype=jnp.int32)
    values = values.reshape(-1).at[chosen].set(ATOM_DEV).reshape(N_CELLS, N_GRP)
    return values.astype(jnp.int32)


def draw_anchor(key, part):
    base_key = jax.random.fold_in(key, 23)
    raw_key, band_key, phase_key, pick_key, spare_key, chosen_key = jax.random.split(base_key, 6)
    raw_values = jax.random.randint(raw_key, (3, N_CELLS, N_GRP, ATOM_DEV), 0, 1048576, dtype=jnp.int32)
    band_width = min(24, GZ // 2)
    swing_depth = min(16, GZ - 1 - band_width)
    band_base = jax.random.randint(band_key, (), 0, GZ - band_width - swing_depth, dtype=jnp.int32)
    phase_shift = jax.random.randint(phase_key, (), 0, 2 * swing_depth, dtype=jnp.int32)
    cell_rows = jnp.arange(N_CELLS, dtype=jnp.int32)[:, None]
    cell_columns = jnp.arange(N_GRP, dtype=jnp.int32)[None, :]
    triangle = jnp.abs((cell_rows + cell_columns + phase_shift) % (2 * swing_depth) - swing_depth)
    in_band = band_base + triangle[:, :, None] + raw_values[2] % band_width
    background = jax.random.randint(spare_key, (N_CELLS, N_GRP, ATOM_DEV), 0, GZ - 1, dtype=jnp.int32)
    picked = jax.random.randint(pick_key, (N_CELLS, N_GRP, ATOM_DEV), 0, 8, dtype=jnp.int32) == 0
    depth_values = jnp.where(picked, background, in_band)
    chosen = jax.random.randint(chosen_key, (), 0, N_CELLS * N_GRP, dtype=jnp.int32)
    depth_values = depth_values.reshape(N_CELLS * N_GRP, ATOM_DEV).at[chosen, 0].set(GZ - 2).reshape(N_CELLS, N_GRP, ATOM_DEV)
    first_values = raw_values[0] % BX
    second_values = raw_values[1] % BYD
    return jnp.stack([first_values, second_values, depth_values]).astype(jnp.int32)


def draw_type_table(key, part):
    amp_key, width_key, mass_key = jax.random.split(jax.random.fold_in(key, 37), 3)
    amplitude = jnp.exp(jax.random.uniform(amp_key, (TYPES,), jnp.float32, jnp.log(0.7), jnp.log(2.0)))
    widths = jax.random.uniform(width_key, (TYPES,), jnp.float32, 1.7, 2.4)
    masses = jnp.exp(jax.random.uniform(mass_key, (TYPES,), jnp.float32, jnp.log(0.7), jnp.log(2.0)))
    return jnp.stack([amplitude, widths, masses]).astype(jnp.float32)


def set_ends(values, own_key, low, top_value):
    place = [jax.random.randint(jax.random.fold_in(own_key, axis), (), 0, length) for axis, length in enumerate(values.shape)]
    widest = values.shape.index(max(values.shape))
    neighbour = place[:widest] + [(place[widest] + 1) % values.shape[widest]] + place[widest + 1:]
    return values.at[tuple(place)].set(low).at[tuple(neighbour)].set(top_value)


def steps_of(key, shape, shards, low, high):
    factor_of = 1.0
    for dim, shards_of in shards:
        draws = jax.random.uniform(jax.random.fold_in(jax.random.fold_in(key, 6), dim), (shards_of,), jnp.float32, low / len(shards), high / len(shards))
        factor_of = factor_of * jnp.repeat(jnp.exp(draws), shape[dim] // shards_of).reshape((-1,) + (1,) * (len(shape) - 1 - dim))
    return factor_of


def gaussian(stream_key, dims, deviation, limit, cuts=(), kind=jnp.bfloat16):
    values = deviation * jax.random.normal(stream_key, dims, jnp.float32)
    if cuts:
        values = values * steps_of(stream_key, dims, cuts, -0.22, 0.18)
    return jnp.clip(values, -limit, limit).astype(kind)


def setup_inputs(seed: int = 0) -> dict:
    keys = jax.random.split(jax.random.key(seed), 8)
    return {
        "fraction": jnp.clip(1.0 * jax.random.uniform(keys[0], (3, N_CELLS, N_GRP, ATOM_DEV), jnp.float32) ** steps_of(keys[0], (3, N_CELLS, N_GRP, ATOM_DEV), ((1, 128), (2, 4)), -0.2, 0.2), 0.0, 1.0),
        "velocity": gaussian(keys[1], (3, N_CELLS, N_GRP, ATOM_DEV), 0.3, 1.8, ((1, 128), (2, 4)), jnp.float32),
        "anchor": draw_anchor(jax.random.fold_in(keys[7], 71), 0),
        "atom_types": set_ends(jax.random.randint(keys[3], (N_CELLS, N_GRP, ATOM_DEV), 0, TYPES), jax.random.fold_in(keys[3], 1), 0, TYPES - 1).astype(jnp.int32),
        "counts": draw_counts(jax.random.fold_in(keys[7], 71), 0),
        "type_table": draw_type_table(jax.random.fold_in(keys[7], 71), 0),
        "target": gaussian(keys[6], (NX, NY, GZ), 0.05, 0.3, ((0, 128), (1, 4)), jnp.float32),
    }


EPSILON = 1e-06
TIME_STEP = 0.5
BLUR_KERNEL = (1.0 / 16.0, 4.0 / 16.0, 6.0 / 16.0, 4.0 / 16.0, 1.0 / 16.0)
BOX_KERNEL = (1.0 / 9.0,) * 9

def tap_valid(values, along_axis, kernel):
    radius = (len(kernel) - 1) // 2
    length = values.shape[along_axis] - 2 * radius
    summed = kernel[0] * lax.slice_in_dim(values, 0, length, axis=along_axis)
    for offset in range(1, len(kernel)):
        summed = summed + kernel[offset] * lax.slice_in_dim(values, offset, offset + length, axis=along_axis)
    return summed

def tap_padded(values, along_axis, kernel):
    radius = (len(kernel) - 1) // 2
    widths = [(0, 0)] * values.ndim
    widths[along_axis] = (radius, radius)
    return tap_valid(jnp.pad(values, widths), along_axis, kernel)

def filter_three(values, kernel):
    return tap_padded(tap_padded(tap_padded(values, 0, kernel), 1, kernel), 2, kernel)

def corner_weights(position, fraction, extent):
    places = jnp.arange(extent, dtype=jnp.float32)
    lower = (position[:, None] == places[None, :]).astype(jnp.float32)
    upper = (position[:, None] + 1.0 == places[None, :]).astype(jnp.float32)
    return (lower * (1.0 - fraction[:, None]) + upper * fraction[:, None], upper - lower)

def spread_brick(anchors, fractions, amounts, extent_x, extent_y, extent_z):
    atom_count = anchors.shape[1]
    weight_x = corner_weights(anchors[0], fractions[0], extent_x)[0]
    weight_y = corner_weights(anchors[1], fractions[1], extent_y)[0]
    weight_z = corner_weights(anchors[2], fractions[2], extent_z)[0]
    plane = (weight_x[:, :, None] * weight_y[:, None, :]).reshape(atom_count, extent_x * extent_y)
    depth = weight_z * amounts[:, None]
    summed = lax.dot_general(plane, depth, (((0,), (0,)), ((), ())), precision=lax.Precision.HIGHEST, preferred_element_type=jnp.float32)
    return summed.reshape(extent_x, extent_y, extent_z)

def sample_gradient(anchors, fractions, field):
    extent_x, extent_y, extent_z = field.shape
    atom_count = anchors.shape[1]
    weight_x, slope_x = corner_weights(anchors[0], fractions[0], extent_x)
    weight_y, slope_y = corner_weights(anchors[1], fractions[1], extent_y)
    weight_z, slope_z = corner_weights(anchors[2], fractions[2], extent_z)
    matrix = field.reshape(extent_x * extent_y, extent_z)
    stacked = jnp.concatenate([weight_z, slope_z], 0)
    product = lax.dot_general(stacked, matrix, (((1,), (1,)), ((), ())), precision=lax.Precision.HIGHEST, preferred_element_type=jnp.float32)
    product = product.reshape(2, atom_count, extent_x, extent_y)
    grad_x = jnp.einsum('ax,ay,axy->a', slope_x, weight_y, product[0], precision=lax.Precision.HIGHEST)
    grad_y = jnp.einsum('ax,ay,axy->a', weight_x, slope_y, product[0], precision=lax.Precision.HIGHEST)
    grad_z = jnp.einsum('ax,ay,axy->a', weight_x, weight_y, product[1], precision=lax.Precision.HIGHEST)
    return jnp.stack([grad_x, grad_y, grad_z])

def pair_block(own, others):
    offsets = own[0:3, :, None] - others[0:3, None, :] + (own[3:6, :, None] - others[3:6, None, :])
    distance = lax.optimization_barrier(jnp.sum(offsets * offsets, 0))
    spread = own[7][:, None] + others[7][None, :]
    coupling = others[6][None, :] * jnp.exp(-0.5 * distance / spread) / spread
    return own[6][None, :] * lax.optimization_barrier(jnp.sum(coupling[None] * offsets, 2))

def type_values(kinds, table):
    matches = (kinds[..., None] == jnp.arange(table.shape[1], dtype=jnp.int32)).astype(jnp.float32)
    shaped = table.reshape((3,) + (1,) * kinds.ndim + (table.shape[1],))
    return lax.optimization_barrier(jnp.sum(matches[None] * shaped, -1))

def cell_pairs(own, others):
    block_size = min(128, own.shape[1])
    blocks = own.reshape(8, -1, block_size).transpose(1, 0, 2)
    result = lax.map(lambda piece: pair_block(piece, others), blocks)
    return result.transpose(1, 0, 2).reshape(3, -1)

def all_pairs(packet):
    padded = jnp.pad(packet, ((0, 0), (1, 1), (1, 1), (0, 0)))

    def per_slab(slab_index):
        window = lax.dynamic_slice(padded, (jnp.int32(0), slab_index, jnp.int32(0), jnp.int32(0)), (8, 3, N_GRP + 2, ATOM_DEV))
        pieces = []
        for quarter in range(N_GRP):
            others = window[:, :, quarter:quarter + 3, :].reshape(8, 9 * ATOM_DEV)
            pieces.append(cell_pairs(window[:, 1, quarter + 1, :], others))
        return jnp.stack(pieces, 1)
    result = lax.map(per_slab, jnp.arange(N_CELLS, dtype=jnp.int32))
    return result.transpose(1, 0, 2, 3)

def full_density(anchor_local, fraction, charge):

    def per_slab(inputs):
        anchors, fractions, amounts = inputs
        return jnp.stack([spread_brick(anchors[:, quarter], fractions[:, quarter], amounts[quarter], BX + 1, BYD + 1, GZ) for quarter in range(N_GRP)])
    bricks = lax.map(per_slab, (jnp.moveaxis(anchor_local, 1, 0), jnp.moveaxis(fraction, 1, 0), charge))
    rows_out = bricks[:, :, BX]
    arrived = jnp.concatenate([jnp.zeros_like(rows_out[:1]), rows_out[:-1]], 0)
    upper = bricks[:, :, :BX].at[:, :, 0].add(arrived)
    columns = upper[:, :, :, BYD]
    arrived_side = jnp.concatenate([jnp.zeros_like(columns[:, :1]), columns[:, :-1]], 1)
    inner = upper[:, :, :, :BYD].at[:, :, :, 0].add(arrived_side)
    return inner.transpose(0, 2, 1, 3, 4).reshape(NX, NY, GZ)

def full_gradient(anchor_local, fraction, field):
    padded = jnp.pad(field, ((0, 1), (0, 1), (0, 0)))

    def per_slab(inputs):
        slab_index, anchors, fractions = inputs
        planes = lax.dynamic_slice_in_dim(padded, slab_index * BX, BX + 1, 0)
        return jnp.stack([sample_gradient(anchors[:, quarter], fractions[:, quarter], planes[:, quarter * BYD:quarter * BYD + BYD + 1]) for quarter in range(N_GRP)], 1)
    result = lax.map(per_slab, (jnp.arange(N_CELLS, dtype=jnp.int32), jnp.moveaxis(anchor_local, 1, 0), jnp.moveaxis(fraction, 1, 0)))
    return result.transpose(1, 0, 2, 3)

def reference(fraction, velocity, anchor, atom_types, counts, type_table, target):
    live = (jnp.arange(ATOM_DEV, dtype=jnp.int32)[None, None, :] < counts[:, :, None]).astype(jnp.float32)
    properties = type_values(atom_types, type_table)
    charge = properties[0] * live
    square_width = properties[1] * properties[1]
    masses = properties[2]
    first_x = jnp.broadcast_to((jnp.arange(N_CELLS, dtype=jnp.int32) * BX)[:, None], (N_CELLS, N_GRP))
    first_y = jnp.broadcast_to((jnp.arange(N_GRP, dtype=jnp.int32) * BYD)[None, :], (N_CELLS, N_GRP))
    root = jnp.stack([first_x, first_y, jnp.zeros((N_CELLS, N_GRP), jnp.int32)])
    anchor_local = anchor.astype(jnp.float32)
    anchor_global = (anchor + root[..., None]).astype(jnp.float32)
    mean_one = filter_three(target, BOX_KERNEL)
    mean_two = filter_three(target * target, BOX_KERNEL)
    inverse_scale = lax.rsqrt(mean_two - mean_one * mean_one + EPSILON)
    moved = jnp.zeros_like(velocity)
    potential = jnp.zeros_like(target)
    for turn_index in range(STEPS):
        packet = jnp.concatenate([anchor_global, fraction, charge[None], square_width[None]], 0)
        forces = all_pairs(packet)
        density = full_density(anchor_local, fraction, charge)
        residual = (filter_three(density, BLUR_KERNEL) - target) * inverse_scale
        potential = filter_three(residual, BLUR_KERNEL)
        gradient = full_gradient(anchor_local, fraction, potential)
        forces = forces - charge[None] * gradient
        velocity = velocity + TIME_STEP * forces / masses[None]
        moved = moved + TIME_STEP * velocity
        fraction = fraction + TIME_STEP * velocity
    return (velocity * live[None], moved * live[None], potential)
```

```python
import functools

import jax
import jax.numpy as jnp
from jax import lax
from jax.experimental import pallas as pl
from jax.experimental.pallas import tpu as pltpu
from jax.sharding import PartitionSpec as P

STEPS = 2
EPSILON = 1e-06
TIME_STEP = 0.5
BLUR = (1.0 / 16.0, 4.0 / 16.0, 6.0 / 16.0, 4.0 / 16.0, 1.0 / 16.0)
KAPPA = 0.8493218002880191
HIGH = lax.Precision.HIGHEST
LANES = 128
I_ROWS = 64


def dot(a, b, dims, precision=HIGH):
    return lax.dot_general(
        a, b, (dims, ((), ())), precision=precision, preferred_element_type=jnp.float32
    )


def split(value):
    high = value.astype(jnp.bfloat16)
    return high, (value - high.astype(jnp.float32)).astype(jnp.bfloat16)


def dot_split(a, b, dims):
    a_high, a_low = split(a)
    b_high, b_low = split(b)
    return dot(a_high, b_high, dims, None) + (
        dot(a_high, b_low, dims, None) + dot(a_low, b_high, dims, None)
    )


def iota(shape, dim):
    return lax.broadcasted_iota(jnp.int32, shape, dim)


def band(radius, weights):
    offset = iota((256, 256), 0) - iota((256, 256), 1)
    result = jnp.zeros((256, 256), jnp.float32)
    for shift in range(-radius, radius + 1):
        result = jnp.where(offset == shift, weights[shift + radius], result)
    return result


def rows_filtered(values, weights):
    radius = (len(weights) - 1) // 2
    result = weights[radius] * values
    for shift in range(1, radius + 1):
        both = pltpu.roll(values, shift, 1) + pltpu.roll(values, values.shape[1] - shift, 1)
        result = result + weights[radius + shift] * both
    return result


def planes_filtered(values, weights, count):
    result = weights[0] * values[0:count]
    for shift in range(1, len(weights)):
        result = result + weights[shift] * values[shift : shift + count]
    return result


def inside(place, first_plane, planes):
    shape = (planes, 32, 256)
    plane = place[0] * 4 + first_plane + iota(shape, 0)
    row = place[1] * 16 - 8 + iota(shape, 1)
    return (plane >= 0) & (plane < place[2]) & (row >= 0) & (row < place[3])


def prep_kernel(counts, table, fraction, velocity, anchor, kinds, atoms, state):
    for half in range(2):
        lanes = pl.ds(half * 256, 256)
        kind = kinds[0, :, lanes]
        live = (iota((1, 256), 1) + half * 256 < counts[0, 0]).astype(jnp.float32)
        values = []
        for row in range(3):
            value = jnp.zeros((1, 256), jnp.float32)
            for option in range(table.shape[1]):
                value = jnp.where(kind == option, table[row, option], value)
            values.append(value)
        for row in range(3):
            atoms[half, row : row + 1, :] = anchor[row, 0, :, lanes].astype(jnp.float32)
            atoms[half, row + 3 : row + 4, :] = fraction[row, 0, :, lanes]
            state[half, row : row + 1, :] = velocity[row, 0, :, lanes]
            state[half, row + 3 : row + 4, :] = jnp.zeros((1, 256), jnp.float32)
        atoms[half, 6:7, :] = values[0] * live
        atoms[half, 7:8, :] = values[1] * values[1]
        state[half, 6:7, :] = values[2]
        state[half, 7:8, :] = live


def scale_kernel(place, target, scale):
    box = (1.0,) * 9
    matrix = band(4, box)
    value = target[2:19]
    sums = []
    for source in (value, value * value):
        summed = rows_filtered(planes_filtered(source, box, 9), box)
        summed = dot(summed.reshape(288, 256), matrix, ((1,), (0,)))
        sums.append(summed.reshape(9, 32, 256) * (1.0 / 729.0))
    result = lax.rsqrt(sums[1] - sums[0] * sums[0] + EPSILON)
    scale[...] = jnp.where(inside(place, -2, 9), result, 0.0)


def step_kernel(
    last, counts, place, atoms, state, target, scale, *refs
):
    if last:
        final_velocity, displacement, potential_out = refs[:3]
    else:
        atoms_out, state_out = refs[:2]
    pair_blocks, spread_blocks, own_columns, sums, density = refs[-5:]

    row_index = iota((8, LANES), 0)
    pair_count = jnp.int32(0)
    spread_counts = []
    for column in range(5):
        spread_count = jnp.int32(0)
        for side in range(3):
            shift = jnp.where(
                row_index == 0,
                4.0 * (column - 2),
                jnp.where(row_index == 1, 16.0 * (side - 1), 0.0),
            )
            for part in range(4):
                block = atoms[column, side, part // 2, :, pl.ds((part % 2) * LANES, LANES)] + shift
                alive = block[6, 0] > 0.0
                spread_blocks[column, spread_count] = block
                spread_count = spread_count + alive.astype(jnp.int32)
                if column in (1, 2, 3):
                    place_of = block[0:3] + block[3:6]
                    pair_blocks[pair_count, 0:3, :] = KAPPA * place_of
                    pair_blocks[pair_count, 3:4, :] = block[6:7]
                    pair_blocks[pair_count, 4:5, :] = block[7:8]
                    pair_count = pair_count + alive.astype(jnp.int32)
        spread_blocks[column, spread_count] = jnp.zeros((8, LANES), jnp.float32)
        spread_counts.append(spread_count)
    pair_blocks[pair_count] = jnp.zeros((8, LANES), jnp.float32)

    for half in range(2):
        own = atoms[2, 1, half]
        packed = jnp.concatenate(
            [KAPPA * (own[0:3] + own[3:6]), own[7:8], jnp.zeros((4, 256), jnp.float32)], 0
        )
        turned = jnp.transpose(packed)
        for row in range(4):
            own_columns[row, pl.ds(half * 256, 256), :] = jnp.broadcast_to(
                turned[:, row : row + 1], (256, LANES)
            )
    sums[...] = jnp.zeros(sums.shape, jnp.float32)

    def add_rows(index, carry):
        rows = pl.ds(index * I_ROWS, I_ROWS)
        own_x, own_y, own_z, own_s = (own_columns[row, rows, :] for row in range(4))

        def add_blocks(step, totals):
            for part in range(2):
                block = pair_blocks[step * 2 + part]
                x = own_x - block[0:1]
                y = own_y - block[1:2]
                z = own_z - block[2:3]
                spread = own_s + block[4:5]
                inverse = pl.reciprocal(spread, approx=True)
                inverse = inverse * (2.0 - spread * inverse)
                squared = x * x + y * y + z * z
                factor = block[3:4] * jnp.exp2(-(squared * inverse)) * inverse
                totals = (totals[0] + factor * x, totals[1] + factor * y, totals[2] + factor * z)
            return totals

        zero = jnp.zeros((I_ROWS, LANES), jnp.float32)
        totals = lax.fori_loop(0, (pair_count + 1) // 2, add_blocks, (zero, zero, zero))
        for axis in range(3):
            sums[axis, rows, :] = totals[axis]
        return carry

    lax.fori_loop(0, (counts[0, 0] + I_ROWS - 1) // I_ROWS, add_rows, 0)

    density[...] = jnp.zeros(density.shape, jnp.float32)
    depth = iota((256, 256), 0).astype(jnp.float32)
    height = iota((32, 256), 0).astype(jnp.float32) - 8.0
    for column in range(5):
        planes = {0: (-4,), 4: (8,)}.get(column) or tuple(range(4 * column - 8, 4 * column - 3))

        def add_chunk(step, carry, column=column, planes=planes):
            chunk = jnp.concatenate(
                [spread_blocks[column, step * 2], spread_blocks[column, step * 2 + 1]], 1
            )
            fx, fy, fz = chunk[3:4], chunk[4:5], chunk[5:6]
            charge = chunk[6:7]
            weight_z = jnp.where(
                depth == chunk[2:3],
                charge * (1.0 - fz),
                jnp.where(depth == chunk[2:3] + 1.0, charge * fz, 0.0),
            )
            weight_y = jnp.where(
                height == chunk[1:2], 1.0 - fy, jnp.where(height == chunk[1:2] + 1.0, fy, 0.0)
            )
            parts = []
            for plane in planes:
                weight_x = jnp.where(
                    chunk[0:1] == plane, 1.0 - fx, jnp.where(chunk[0:1] + 1.0 == plane, fx, 0.0)
                )
                parts.append(weight_x * weight_y)
            added = dot_split(jnp.concatenate(parts, 0), weight_z, ((1,), (1,)))
            where = pl.ds(planes[0] + 4, len(planes))
            density[where] = density[where] + added.reshape(len(planes), 32, 256)
            return carry

        lax.fori_loop(0, (spread_counts[column] + 1) // 2, add_chunk, 0)

    matrix = band(2, BLUR)
    value = jnp.where(inside(place, -4, 13), density[...], 0.0)
    value = rows_filtered(planes_filtered(value, BLUR, 9), BLUR)
    value = dot(value.reshape(288, 256), matrix, ((1,), (0,))).reshape(9, 32, 256)
    residual = (value - target[6:15]) * scale[...]
    value = rows_filtered(planes_filtered(residual, BLUR, 5), BLUR)
    value = dot(value.reshape(160, 256), matrix, ((1,), (0,))).reshape(5, 32, 256)
    potential = jnp.where(inside(place, 0, 5), value, 0.0)
    if last:
        potential_out[...] = potential[0:4, 8:24]
    field = potential[:, 8:32].reshape(120, 256)

    ones = jnp.ones((8, LANES), jnp.float32)
    height = iota((24, 256), 0).astype(jnp.float32)
    for half in range(2):
        own = atoms[2, 1, half]
        gx, gy, gz, fx, fy, fz = (own[row : row + 1] for row in range(6))
        lower, upper = depth == gz, depth == gz + 1.0
        product = dot_split(
            field, jnp.where(lower, 1.0 - fz, jnp.where(upper, fz, 0.0)), ((1,), (0,))
        ).reshape(5, 24, 256)
        slope = jnp.where(lower, -1.0, jnp.where(upper, 1.0, 0.0))
        product_z = dot_split(field, slope, ((1,), (0,))).reshape(5, 24, 256)
        lower, upper = height == gy, height == gy + 1.0
        weight_y = jnp.where(lower, 1.0 - fy, jnp.where(upper, fy, 0.0))
        slope_y = jnp.where(lower, -1.0, jnp.where(upper, 1.0, 0.0))
        mixed = [jnp.zeros((24, 256), jnp.float32) for _ in range(3)]
        for plane in range(5):
            lower, upper = gx == plane, gx + 1.0 == plane
            weight_x = jnp.where(lower, 1.0 - fx, jnp.where(upper, fx, 0.0))
            slope_x = jnp.where(lower, -1.0, jnp.where(upper, 1.0, 0.0))
            mixed[0] = mixed[0] + slope_x * product[plane]
            mixed[1] = mixed[1] + weight_x * product[plane]
            mixed[2] = mixed[2] + weight_x * product_z[plane]
        gradient = (
            jnp.sum(mixed[0] * weight_y, 0, keepdims=True),
            jnp.sum(mixed[1] * slope_y, 0, keepdims=True),
            jnp.sum(mixed[2] * weight_y, 0, keepdims=True),
        )
        charge = own[6:7]
        values = state[half]
        mass, live = values[6:7], values[7:8]
        if not last:
            atoms_out[half, 6:8, :] = own[6:8]
            atoms_out[half, 0:3, :] = own[0:3]
            state_out[half, 6:8, :] = values[6:8]
        for axis in range(3):
            pair = dot(ones, sums[axis, pl.ds(half * 256, 256), :], ((1,), (1,)))[0:1]
            force = charge * (pair * (1.0 / KAPPA) - gradient[axis])
            velocity = values[axis : axis + 1] + TIME_STEP * force / mass
            moved = values[axis + 3 : axis + 4] + TIME_STEP * velocity
            if last:
                lanes = pl.ds(half * 256, 256)
                final_velocity[axis, 0, :, lanes] = velocity * live
                displacement[axis, 0, :, lanes] = moved * live
            else:
                state_out[half, axis : axis + 1, :] = velocity
                state_out[half, axis + 3 : axis + 4, :] = moved
                atoms_out[half, axis + 3 : axis + 4, :] = (
                    own[axis + 3 : axis + 4] + TIME_STEP * velocity
                )


SMEM = pl.BlockSpec(memory_space=pltpu.SMEM)
VMEM = pl.BlockSpec(memory_space=pltpu.VMEM)


def shape(*dims):
    return jax.ShapeDtypeStruct(dims, jnp.float32)


def links():
    chips = lax.axis_size("cells") // 2
    groups = lax.axis_size("grp")

    def coloured(count, first):
        pairs = []
        for left in range(first, count - 1, 2):
            pairs += [(left, left + 1), (left + 1, left)]
        return pairs

    def doubled(pairs):
        return [(2 * a + core, 2 * b + core) for a, b in pairs for core in range(2)]

    return {
        "odd": ("cells", doubled(coloured(chips, 1))),
        "even": ("cells", doubled(coloured(chips, 0))),
        "rows_even": ("grp", coloured(groups, 0)),
        "rows_odd": ("grp", coloured(groups, 1)),
        "pair": ("cells", [(i, i ^ 1) for i in range(2 * chips)]),
    }


def spread_out(own, rows, groups, flags):
    even_chip, even_row, first_core = flags

    def send(value, link):
        return lax.ppermute(value, *groups[link])

    odd = send(own, "odd")
    even = send(own, "even")
    left = jnp.where(even_chip, odd, even)
    right = jnp.where(even_chip, even, odd)
    columns = jnp.stack([own, left, right])
    from_even = send(rows(columns, even_row), "rows_even")
    from_odd = send(rows(columns, ~even_row), "rows_odd")
    above = jnp.where(even_row, from_even, from_odd)
    below = jnp.where(even_row, from_odd, from_even)
    return columns, below, above, functools.partial(send, link="pair")


def finish(full, send, first_core):
    chosen = jnp.where(first_core, full[2], full[1])
    got = send(jnp.stack([full[0], chosen]))
    minus = jnp.where(first_core, got[1], got[0])
    plus = jnp.where(first_core, got[0], got[1])
    return jnp.stack([full[1], minus, full[0], plus, full[2]])


def per_device(fraction, velocity, anchor, atom_types, counts, type_table, target):
    cells, groups_count = lax.axis_size("cells"), lax.axis_size("grp")
    cell, group = lax.axis_index("cells"), lax.axis_index("grp")
    groups = links()
    flags = ((cell // 2) % 2 == 0, group % 2 == 0, cell % 2 == 0)
    place = jnp.stack(
        [cell, group, jnp.int32(cells * 4), jnp.int32(groups_count * 16)]
    ).astype(jnp.int32)

    atoms, state = pl.pallas_call(
        prep_kernel,
        out_shape=(shape(2, 8, 256), shape(2, 8, 256)),
        in_specs=[SMEM, SMEM, VMEM, VMEM, VMEM, VMEM],
        out_specs=(VMEM, VMEM),
        name="prep",
    )(counts, type_table, fraction, velocity, anchor, atom_types)

    def rows_first(columns, upper):
        fields = columns[:, 2:].reshape(3, 4, 2, 8, 256)
        return jnp.concatenate(
            [columns[:, :2], jnp.where(upper, fields[:, :, 1], fields[:, :, 0])], 1
        )

    own = jnp.concatenate([atoms, target.reshape(8, 8, 256)], 0)
    columns, below, above, send = spread_out(own, rows_first, groups, flags)
    full = jnp.concatenate(
        [
            jnp.stack([below[:, :2], columns[:, :2], above[:, :2]], 1).reshape(3, 6, 8, 256),
            jnp.concatenate(
                [
                    below[:, 2:, None],
                    columns[:, 2:].reshape(3, 4, 2, 8, 256),
                    above[:, 2:, None],
                ],
                2,
            ).reshape(3, 16, 8, 256),
        ],
        1,
    )
    full = finish(full, send, flags[2])
    near = full[:, :6].reshape(5, 3, 2, 8, 256)
    wide = full[:, 6:].reshape(20, 32, 256)

    scale = pl.pallas_call(
        scale_kernel,
        out_shape=shape(9, 32, 256),
        in_specs=[SMEM, VMEM],
        out_specs=VMEM,
        name="scale",
    )(place, wide)

    scratch = [
        pltpu.VMEM((38, 8, LANES), jnp.float32),
        pltpu.VMEM((5, 14, 8, LANES), jnp.float32),
        pltpu.VMEM((4, 512, LANES), jnp.float32),
        pltpu.VMEM((3, 512, LANES), jnp.float32),
        pltpu.VMEM((13, 32, 256), jnp.float32),
    ]
    for turn in range(STEPS):
        last = turn == STEPS - 1
        if last:
            outs = (shape(*velocity.shape), shape(*velocity.shape), shape(*target.shape))
        else:
            outs = (shape(2, 8, 256), shape(2, 8, 256))
        result = pl.pallas_call(
            functools.partial(step_kernel, last),
            out_shape=outs,
            in_specs=[SMEM, SMEM, VMEM, VMEM, VMEM, VMEM],
            out_specs=(VMEM,) * len(outs),
            scratch_shapes=scratch,
            name="step_last" if last else "step",
        )(counts, place, near, state, wide, scale)
        if last:
            return result
        atoms, state = result
        columns, below, above, send = spread_out(atoms, lambda c, upper: c, groups, flags)
        full = jnp.stack([below, columns, above], 1)
        near = finish(full, send, flags[2])


def solution(mesh):
    placed = (
        P(None, "cells", "grp", None),
        P(None, "cells", "grp", None),
        P(None, "cells", "grp", None),
        P("cells", "grp", None),
        P("cells", "grp"),
        P(),
        P("cells", "grp", None),
    )
    return jax.shard_map(
        per_device,
        mesh=mesh,
        in_specs=placed,
        out_specs=(
            P(None, "cells", "grp", None),
            P(None, "cells", "grp", None),
            P("cells", "grp", None),
        ),
        check_vma=False,
    )
```

```python
import functools

import jax
import jax.numpy as jnp
from jax import lax
from jax.experimental import pallas as pl
from jax.experimental.pallas import tpu as pltpu
from jax.sharding import PartitionSpec as P

STEPS = 2
EPSILON = 1e-06
TIME_STEP = 0.5
BLUR = (1.0 / 16.0, 4.0 / 16.0, 6.0 / 16.0, 4.0 / 16.0, 1.0 / 16.0)
KAPPA = 0.8493218002880191
LANES = 128
I_ROWS = 64


def dot(a, b, dims, precision=None):
    return lax.dot_general(
        a, b, (dims, ((), ())), precision=precision, preferred_element_type=jnp.float32
    )


def split(value, pieces):
    parts = []
    for _ in range(pieces):
        parts.append(value.astype(jnp.bfloat16))
        value = value - parts[-1].astype(jnp.float32)
    return parts


def dot_exact(a, b, dims, pieces=2):
    total = None
    for part in reversed(split(a, pieces)):
        product = dot(part, b, dims)
        total = product if total is None else total + product
    return total


def iota(shape, dim):
    return lax.broadcasted_iota(jnp.int32, shape, dim)


def band(weights):
    radius = (len(weights) - 1) // 2
    offset = iota((256, 256), 0) - iota((256, 256), 1)
    result = jnp.zeros((256, 256), jnp.float32)
    for shift in range(-radius, radius + 1):
        result = jnp.where(offset == shift, weights[shift + radius], result)
    return result.astype(jnp.bfloat16)


def rows_filtered(values, weights):
    radius = (len(weights) - 1) // 2
    result = weights[radius] * values
    for shift in range(1, radius + 1):
        both = pltpu.roll(values, shift, 1) + pltpu.roll(values, values.shape[1] - shift, 1)
        result = result + weights[radius + shift] * both
    return result


def rows_boxed(values):
    pairs = values + pltpu.roll(values, 1, 1)
    fours = pairs + pltpu.roll(pairs, 2, 1)
    eights = fours + pltpu.roll(fours, 4, 1)
    nines = eights + pltpu.roll(values, 8, 1)
    return pltpu.roll(nines, values.shape[1] - 4, 1)


def depth_filtered(values, matrix, pieces):
    flat = values.reshape(values.shape[0] * 32, 256)
    return dot_exact(flat, matrix, ((1,), (0,)), pieces).reshape(values.shape)


def planes_filtered(values, weights, count):
    result = weights[0] * values[0:count]
    for shift in range(1, len(weights)):
        result = result + weights[shift] * values[shift : shift + count]
    return result


def plane_inside(place, plane):
    position = place[0] * 4.0 + plane
    return ((position >= 0.0) & (position < place[2])).astype(jnp.float32)


def rows_inside(place, first, rows):
    position = place[1] * 16.0 + first + iota((rows, 256), 0).astype(jnp.float32)
    return (position >= 0.0) & (position < place[3])


def prep_kernel(
    counts, table, fraction_in, velocity_in, anchor_in, kinds_in, target_in, sent, state,
    fraction, velocity, anchor, kinds, target, sems,
):
    pairs = ((fraction_in, fraction), (velocity_in, velocity), (anchor_in, anchor))
    pairs += ((kinds_in, kinds), (target_in, target))
    copies = [pltpu.make_async_copy(*pair, sems.at[i]) for i, pair in enumerate(pairs)]
    for copy in copies:
        copy.start()
    info = (lax.axis_index("cells"), lax.axis_index("grp"), counts[0, 0])
    for row, value in enumerate(info):
        state[2, row : row + 1, :] = jnp.full((1, 256), value, jnp.int32).astype(jnp.float32)
    state[2, 3:8, :] = jnp.zeros((5, 256), jnp.float32)
    for copy in copies:
        copy.wait()
    for half in range(2):
        lanes = pl.ds(half * 256, 256)
        kind = kinds[0, :, lanes]
        live = (iota((1, 256), 1) + half * 256 < counts[0, 0]).astype(jnp.float32)
        values = []
        for row in range(3):
            value = jnp.zeros((1, 256), jnp.float32)
            for option in range(table.shape[1]):
                value = jnp.where(kind == option, table[row, option], value)
            values.append(value)
        for row in range(3):
            sent[half, row : row + 1, :] = anchor[row, 0, :, lanes].astype(jnp.float32)
            sent[half, row + 3 : row + 4, :] = fraction[row, 0, :, lanes]
            state[half, row : row + 1, :] = velocity[row, 0, :, lanes]
            state[half, row + 3 : row + 4, :] = jnp.zeros((1, 256), jnp.float32)
        sent[half, 6:7, :] = values[0] * live
        sent[half, 7:8, :] = values[1] * values[1]
        state[half, 6:7, :] = values[2]
        state[half, 7:8, :] = live
    for plane in range(4):
        for half in range(2):
            sent[2 + 2 * plane + half] = target[plane, pl.ds(8 * half, 8), :]


def inverse_scale(place, full, scale, scaled):
    matrix = band((1.0,) * 9)
    rows = rows_inside(place, -8, 32)
    planes = [full[index // 4, pl.ds(6 + index % 4 * 4, 4)] for index in range(2, 19)]
    planes = jnp.stack([plane.reshape(32, 256) for plane in planes])
    sums = []
    for source in (planes, planes * planes):
        pairs = source[0:16] + source[1:17]
        fours = pairs[0:14] + pairs[2:16]
        summed = fours[0:9] + fours[4:13] + source[8:17]
        sums.append(depth_filtered(rows_boxed(summed), matrix, 3) * (1.0 / 729.0))
    value = lax.rsqrt(sums[1] - sums[0] * sums[0] + EPSILON)
    for plane in range(9):
        kept = jnp.where(rows, value[plane], 0.0) * plane_inside(place, plane - 2)
        scale[plane] = kept
        scaled[plane] = kept * planes[plane + 4]


def step_kernel(last, extent, full, state, *refs):
    place = (state[2, 0:1, :], state[2, 1:2, :], *extent)
    count = state[2, 2, 0].astype(jnp.int32)
    if last:
        fractions, scale, scaled, final_velocity, displacement, potential_out = refs[:6]
    else:
        fractions_out, state_out, scale, scaled = refs[:4]
    pair_blocks, spread_blocks, own_columns, sums, density = refs[-5:]
    density[...] = jnp.zeros(density.shape, jnp.float32)
    sums[...] = jnp.zeros(sums.shape, jnp.float32)

    def block_of(column, index, lanes):
        block = full[column, index, :, lanes]
        if last:
            moved = fractions[column, index // 2, index % 2, :, lanes]
            return jnp.concatenate([block[0:3], moved[0:3], block[6:8]], 0)
        return block

    row_index = iota((8, LANES), 0)
    pair_count = jnp.int32(0)
    spread_counts = []
    for column in range(5):
        spread_count = jnp.int32(0)
        for side in range(3):
            shift = jnp.where(
                row_index == 0,
                4.0 * (column - 2),
                jnp.where(row_index == 1, 16.0 * (side - 1), 0.0),
            )
            for part in range(4):
                lanes = pl.ds((part % 2) * LANES, LANES)
                block = block_of(column, side * 2 + part // 2, lanes) + shift
                alive = block[6, 0] > 0.0
                spread_blocks[column, spread_count] = block
                spread_count = spread_count + alive.astype(jnp.int32)
                if column in (1, 2, 3):
                    pair_blocks[pair_count, 0:3, :] = KAPPA * (block[0:3] + block[3:6])
                    pair_blocks[pair_count, 3:4, :] = -block[6:7]
                    pair_blocks[pair_count, 4:5, :] = block[7:8]
                    pair_count = pair_count + alive.astype(jnp.int32)
        spread_blocks[column, spread_count] = jnp.zeros((8, LANES), jnp.float32)
        spread_counts.append(spread_count)
    pair_blocks[pair_count] = jnp.zeros((8, LANES), jnp.float32)

    own_halves = []
    for half in range(2):
        own = jnp.concatenate([block_of(2, 2 + half, pl.ds(i * LANES, LANES)) for i in range(2)], 1)
        own_halves.append(own)
        packed = jnp.concatenate(
            [KAPPA * (own[0:3] + own[3:6]), own[7:8], jnp.zeros((4, 256), jnp.float32)], 0
        )
        turned = jnp.transpose(packed)
        rows = pl.ds(half * 256, 256)
        for row in range(3):
            own_columns[row, rows, :] = jnp.broadcast_to(turned[:, row : row + 1], (256, LANES))
        own_columns[3, rows, :] = jnp.broadcast_to(-turned[:, 3:4], (256, LANES))

    def add_rows(index, carry):
        rows = pl.ds(index * I_ROWS, I_ROWS)
        own_x, own_y, own_z, own_s = (own_columns[row, rows, :] for row in range(4))

        def add_blocks(step, totals):
            for part in range(2):
                block = pair_blocks[step * 2 + part]
                x = own_x - block[0:1]
                y = own_y - block[1:2]
                z = own_z - block[2:3]
                spread = own_s - block[4:5]
                inverse = 1.0 / spread
                factor = jnp.exp2((x * x + y * y + z * z) * inverse)
                factor = (factor * block[3:4]) * inverse
                totals = (totals[0] + factor * x, totals[1] + factor * y, totals[2] + factor * z)
            return totals

        zero = jnp.zeros((I_ROWS, LANES), jnp.float32)
        totals = lax.fori_loop(0, (pair_count + 1) // 2, add_blocks, (zero, zero, zero))
        for axis in range(3):
            sums[axis, rows, :] = totals[axis]
        return carry

    lax.fori_loop(0, (count + I_ROWS - 1) // I_ROWS, add_rows, 0)

    depth = iota((256, 256), 0).astype(jnp.float32)
    height = iota((32, 256), 0).astype(jnp.float32) - 8.0
    rows = rows_inside(place, -8, 32)
    for column in range(5):
        planes = {0: (-4,), 4: (8,)}.get(column) or tuple(range(4 * column - 8, 4 * column - 3))

        def add_chunk(step, carry, column=column, planes=planes):
            chunk = jnp.concatenate(
                [spread_blocks[column, step * 2], spread_blocks[column, step * 2 + 1]], 1
            )
            fx, fy, fz = chunk[3:4], chunk[4:5], chunk[5:6]
            charge = chunk[6:7]
            selected = jnp.where(depth == chunk[2:3], 1.0, 0.0).astype(jnp.bfloat16)
            weight_y = jnp.where(
                height == chunk[1:2], 1.0 - fy, jnp.where(height == chunk[1:2] + 1.0, fy, 0.0)
            )
            weight_y = jnp.where(rows, weight_y, 0.0)
            where = pl.ds(planes[0] + 4, len(planes))
            for part, amount in enumerate((charge * (1.0 - fz), charge * fz)):
                weights = []
                for plane in planes:
                    weight_x = jnp.where(
                        chunk[0:1] == plane, 1.0 - fx, jnp.where(chunk[0:1] + 1.0 == plane, fx, 0.0)
                    )
                    weights.append((weight_x * amount * plane_inside(place, plane)) * weight_y)
                added = dot_exact(jnp.concatenate(weights, 0), selected, ((1,), (1,)))
                density[part, where] = density[part, where] + added.reshape(len(planes), 32, 256)
            return carry

        lax.fori_loop(0, (spread_counts[column] + 1) // 2, add_chunk, 0)

    if not last:
        inverse_scale(place, full, scale, scaled)
    matrix = band(BLUR)
    value = [planes_filtered(density[part], BLUR, 9) for part in range(2)]
    value = value[0] + pltpu.roll(value[1], 1, 2)
    value = depth_filtered(rows_filtered(value, BLUR), matrix, 2)
    residual = value * scale[...] - scaled[...]
    value = rows_filtered(planes_filtered(residual, BLUR, 5), BLUR)
    potential = depth_filtered(value, matrix, 2)
    if last:
        potential_out[...] = potential[0:4, 8:24]

    field = potential[:, 8:32].reshape(120, 256)
    both = split(jnp.concatenate([field, pltpu.roll(field, 255, 1)], 0), 2)
    ones = jnp.ones((8, LANES), jnp.bfloat16)
    height = iota((24, 256), 0).astype(jnp.float32)
    rows = rows_inside(place, 0, 24)
    edge = plane_inside(place, 4)
    for half in range(2):
        own = own_halves[half]
        gx, gy, gz, fx, fy, fz = (own[row : row + 1] for row in range(6))
        selected = jnp.where(depth == gz, 1.0, 0.0).astype(jnp.bfloat16)
        taken = dot(both[0], selected, ((1,), (0,))) + dot(both[1], selected, ((1,), (0,)))
        taken = taken.reshape(2, 5, 24, 256)
        lower, upper = (height == gy) & rows, (height == gy + 1.0) & rows
        weight_y = jnp.where(lower, 1.0 - fy, jnp.where(upper, fy, 0.0))
        slope_y = jnp.where(lower, -1.0, jnp.where(upper, 1.0, 0.0))
        mixed = [jnp.zeros((24, 256), jnp.float32) for _ in range(3)]
        for plane in range(5):
            slope_z = taken[1, plane] - taken[0, plane]
            product = taken[0, plane] + fz * slope_z
            lower, upper = gx == plane, gx + 1.0 == plane
            weight_x = jnp.where(lower, 1.0 - fx, jnp.where(upper, fx, 0.0))
            slope_x = jnp.where(lower, -1.0, jnp.where(upper, 1.0, 0.0))
            if plane == 4:
                weight_x, slope_x = weight_x * edge, slope_x * edge
            mixed[0] = mixed[0] + slope_x * product
            mixed[1] = mixed[1] + weight_x * product
            mixed[2] = mixed[2] + weight_x * slope_z
        gradient = (
            jnp.sum(mixed[0] * weight_y, 0, keepdims=True),
            jnp.sum(mixed[1] * slope_y, 0, keepdims=True),
            jnp.sum(mixed[2] * weight_y, 0, keepdims=True),
        )
        charge = own[6:7]
        values = state[half]
        mass, live = values[6:7], values[7:8]
        if not last:
            state_out[half, 6:8, :] = values[6:8]
            state_out[2] = state[2]
            fractions_out[half, 3:4, :] = jnp.zeros((1, 256), jnp.float32)
        for axis in range(3):
            parts = split(sums[axis, pl.ds(half * 256, 256), :], 2)
            pair = dot(ones, parts[0], ((1,), (1,))) + dot(ones, parts[1], ((1,), (1,)))
            force = charge * (pair[0:1] * (1.0 / KAPPA) - gradient[axis])
            velocity = values[axis : axis + 1] + TIME_STEP * force / mass
            moved = values[axis + 3 : axis + 4] + TIME_STEP * velocity
            if last:
                lanes = pl.ds(half * 256, 256)
                final_velocity[axis, 0, :, lanes] = velocity * live
                displacement[axis, 0, :, lanes] = moved * live
            else:
                state_out[half, axis : axis + 1, :] = velocity
                state_out[half, axis + 3 : axis + 4, :] = moved
                fractions_out[half, axis : axis + 1, :] = (
                    own[axis + 3 : axis + 4] + TIME_STEP * velocity
                )


SMEM = pl.BlockSpec(memory_space=pltpu.SMEM)
VMEM = pl.BlockSpec(memory_space=pltpu.VMEM)
HBM = pl.BlockSpec(memory_space=pltpu.HBM)


def shape(*dims):
    return jax.ShapeDtypeStruct(dims, jnp.float32)


def links():
    chips = lax.axis_size("cells") // 2
    groups = lax.axis_size("grp")

    def coloured(count, first):
        pairs = []
        for left in range(first, count - 1, 2):
            pairs += [(left, left + 1), (left + 1, left)]
        return pairs

    def doubled(pairs):
        return [(2 * a + core, 2 * b + core) for a, b in pairs for core in range(2)]

    return {
        "odd": ("cells", doubled(coloured(chips, 1))),
        "even": ("cells", doubled(coloured(chips, 0))),
        "rows_even": ("grp", coloured(groups, 0)),
        "rows_odd": ("grp", coloured(groups, 1)),
        "pair": ("cells", [(i, i ^ 1) for i in range(2 * chips)]),
    }


def spread_out(own, rows, groups, flags):
    even_chip, even_row, first_core = flags

    def send(value, link):
        return lax.ppermute(value, *groups[link])

    odd = send(own, "odd")
    even = send(own, "even")
    left = jnp.where(even_chip, odd, even)
    right = jnp.where(even_chip, even, odd)
    columns = jnp.stack([own, left, right])
    from_even = send(rows(columns, even_row), "rows_even")
    from_odd = send(rows(columns, ~even_row), "rows_odd")
    above = jnp.where(even_row, from_even, from_odd)
    below = jnp.where(even_row, from_odd, from_even)
    return columns, below, above, functools.partial(send, link="pair")


def finish(full, send, first_core):
    chosen = jnp.where(first_core, full[2], full[1])
    got = send(jnp.stack([full[0], chosen]))
    minus = jnp.where(first_core, got[1], got[0])
    plus = jnp.where(first_core, got[0], got[1])
    return jnp.stack([full[1], minus, full[0], plus, full[2]])


def per_device(fraction, velocity, anchor, atom_types, counts, type_table, target):
    cells, groups_count = lax.axis_size("cells"), lax.axis_size("grp")
    cell, group = lax.axis_index("cells"), lax.axis_index("grp")
    groups = links()
    flags = ((cell // 2) % 2 == 0, group % 2 == 0, cell % 2 == 0)
    extent = (4.0 * cells, 16.0 * groups_count)

    own, state = pl.pallas_call(
        prep_kernel,
        out_shape=(shape(10, 8, 256), shape(3, 8, 256)),
        in_specs=[SMEM, SMEM, HBM, HBM, HBM, HBM, HBM],
        out_specs=(VMEM, VMEM),
        scratch_shapes=[
            pltpu.VMEM(fraction.shape, jnp.float32),
            pltpu.VMEM(velocity.shape, jnp.float32),
            pltpu.VMEM(anchor.shape, jnp.int32),
            pltpu.VMEM(atom_types.shape, jnp.int32),
            pltpu.VMEM(target.shape, jnp.float32),
            pltpu.SemaphoreType.DMA((5,)),
        ],
        name="prep",
    )(counts, type_table, fraction, velocity, anchor, atom_types, target)

    def rows_first(columns, upper):
        fields = columns[:, 2:].reshape(3, 4, 2, 8, 256)
        return jnp.concatenate(
            [columns[:, :2], jnp.where(upper, fields[:, :, 1], fields[:, :, 0])], 1
        )

    columns, below, above, send = spread_out(own, rows_first, groups, flags)
    full = jnp.concatenate(
        [
            jnp.stack([below[:, :2], columns[:, :2], above[:, :2]], 1).reshape(3, 6, 8, 256),
            jnp.concatenate(
                [
                    below[:, 2:, None],
                    columns[:, 2:].reshape(3, 4, 2, 8, 256),
                    above[:, 2:, None],
                ],
                2,
            ).reshape(3, 16, 8, 256),
        ],
        1,
    )
    full = finish(full, send, flags[2])

    field = shape(9, 32, 256)
    scratch = [
        pltpu.VMEM((38, 8, LANES), jnp.float32),
        pltpu.VMEM((5, 14, 8, LANES), jnp.float32),
        pltpu.VMEM((4, 512, LANES), jnp.float32),
        pltpu.VMEM((3, 512, LANES), jnp.float32),
        pltpu.VMEM((2, 13, 32, 256), jnp.float32),
    ]
    fractions, state, scale, scaled = pl.pallas_call(
        functools.partial(step_kernel, False, extent),
        out_shape=(shape(2, 4, 256), shape(3, 8, 256), field, field),
        in_specs=[VMEM, VMEM],
        out_specs=(VMEM,) * 4,
        scratch_shapes=scratch,
        name="step",
        compiler_params=pltpu.CompilerParams(vmem_limit_bytes=24 << 20),
    )(full, state)

    columns, below, above, send = spread_out(fractions, lambda c, upper: c, groups, flags)
    moved = finish(jnp.stack([below, columns, above], 1), send, flags[2])
    return pl.pallas_call(
        functools.partial(step_kernel, True, extent),
        out_shape=(shape(*velocity.shape), shape(*velocity.shape), shape(*target.shape)),
        in_specs=[VMEM] * 5,
        out_specs=(VMEM,) * 3,
        scratch_shapes=scratch,
        name="step_last",
        compiler_params=pltpu.CompilerParams(vmem_limit_bytes=24 << 20),
    )(full, state, moved, scale, scaled)


def solution(mesh):
    placed = (
        P(None, "cells", "grp", None),
        P(None, "cells", "grp", None),
        P(None, "cells", "grp", None),
        P("cells", "grp", None),
        P("cells", "grp"),
        P(),
        P("cells", "grp", None),
    )
    return jax.shard_map(
        per_device,
        mesh=mesh,
        in_specs=placed,
        out_specs=(
            P(None, "cells", "grp", None),
            P(None, "cells", "grp", None),
            P("cells", "grp", None),
        ),
        check_vma=False,
    )
```

```python
import functools

import jax
import jax.numpy as jnp
from jax import lax
from jax.experimental import pallas as pl
from jax.experimental.pallas import tpu as pltpu
from jax.sharding import PartitionSpec as P


EPSILON = 1e-06
TIME_STEP = 0.5
BLUR = (1.0 / 16.0, 4.0 / 16.0, 6.0 / 16.0, 4.0 / 16.0, 1.0 / 16.0)
KAPPA = 0.8493218002880191
LANES = 128
I_ROWS = 64


def dot(a, b, dims, precision=None):
    return lax.dot_general(
        a, b, (dims, ((), ())), precision=precision, preferred_element_type=jnp.float32
    )


def split(value, pieces):
    parts = []
    for _ in range(pieces):
        parts.append(value.astype(jnp.bfloat16))
        value = value - parts[-1].astype(jnp.float32)
    return parts


def dot_exact(a, b, dims, pieces=2):
    count = a.shape[0]
    product = dot(jnp.concatenate(split(a, pieces), 0), b, dims)
    total = product[count * (pieces - 1) :]
    for piece in reversed(range(pieces - 1)):
        total = total + product[count * piece : count * (piece + 1)]
    return total


def iota(shape, dim):
    return lax.broadcasted_iota(jnp.int32, shape, dim)


def band(weights):
    radius = (len(weights) - 1) // 2
    offset = iota((256, 256), 0) - iota((256, 256), 1)
    result = jnp.zeros((256, 256), jnp.float32)
    for shift in range(-radius, radius + 1):
        result = jnp.where(offset == shift, weights[shift + radius], result)
    return result.astype(jnp.bfloat16)


def rows_filtered(values, weights):
    radius = (len(weights) - 1) // 2
    result = weights[radius] * values
    for shift in range(1, radius + 1):
        both = pltpu.roll(values, shift, 1) + pltpu.roll(values, values.shape[1] - shift, 1)
        result = result + weights[radius + shift] * both
    return result


def rows_boxed(values):
    pairs = values + pltpu.roll(values, 1, 1)
    fours = pairs + pltpu.roll(pairs, 2, 1)
    eights = fours + pltpu.roll(fours, 4, 1)
    nines = eights + pltpu.roll(values, 8, 1)
    return pltpu.roll(nines, values.shape[1] - 4, 1)


def depth_filtered(values, matrix, pieces):
    flat = values.reshape(values.shape[0] * 32, 256)
    return dot_exact(flat, matrix, ((1,), (0,)), pieces).reshape(values.shape)


def planes_filtered(values, weights, count):
    result = weights[0] * values[0:count]
    for shift in range(1, len(weights)):
        result = result + weights[shift] * values[shift : shift + count]
    return result


def plane_inside(place, plane):
    position = place[0] * 4.0 + plane
    return ((position >= 0.0) & (position < place[2])).astype(jnp.float32)


def rows_inside(place, first, rows):
    position = place[1] * 16.0 + first + iota((rows, 256), 0).astype(jnp.float32)
    return (position >= 0.0) & (position < place[3])


def prep_kernel(counts, table, fraction, velocity, anchor, kinds, target, sent, state):
    info = (lax.axis_index("cells"), lax.axis_index("grp"), counts[0, 0])
    for row, value in enumerate(info):
        state[2, row : row + 1, :] = jnp.full((1, 256), value, jnp.int32).astype(jnp.float32)
    state[2, 3:8, :] = jnp.zeros((5, 256), jnp.float32)
    for half in range(2):
        lanes = pl.ds(half * 256, 256)
        kind = kinds[0, :, lanes]
        live = (iota((1, 256), 1) + half * 256 < counts[0, 0]).astype(jnp.float32)
        values = []
        for row in range(3):
            value = jnp.zeros((1, 256), jnp.float32)
            for option in range(table.shape[1]):
                value = jnp.where(kind == option, table[row, option], value)
            values.append(value)
        for row in range(3):
            sent[half, row : row + 1, :] = anchor[row, 0, :, lanes].astype(jnp.float32)
            sent[half, row + 3 : row + 4, :] = fraction[row, 0, :, lanes]
            state[half, row : row + 1, :] = velocity[row, 0, :, lanes]
            state[half, row + 3 : row + 4, :] = jnp.zeros((1, 256), jnp.float32)
        sent[half, 6:7, :] = values[0] * live
        sent[half, 7:8, :] = values[1] * values[1]
        state[half, 6:7, :] = values[2]
        state[half, 7:8, :] = live
    for plane in range(4):
        for half in range(2):
            sent[2 + 2 * plane + half] = target[plane, pl.ds(8 * half, 8), :]


def inverse_scale(place, full, scale, scaled):
    matrix = band((1.0,) * 9)
    rows = rows_inside(place, -8, 32)
    planes = [full[index // 4, pl.ds(6 + index % 4 * 4, 4)] for index in range(2, 19)]
    planes = jnp.stack([plane.reshape(32, 256) for plane in planes])
    sums = []
    for source in (planes, planes * planes):
        pairs = source[0:16] + source[1:17]
        fours = pairs[0:14] + pairs[2:16]
        summed = fours[0:9] + fours[4:13] + source[8:17]
        sums.append(depth_filtered(rows_boxed(summed), matrix, 3) * (1.0 / 729.0))
    value = lax.rsqrt(sums[1] - sums[0] * sums[0] + EPSILON)
    for plane in range(9):
        kept = jnp.where(rows, value[plane], 0.0) * plane_inside(place, plane - 2)
        scale[plane] = kept
        scaled[plane] = kept * planes[plane + 4]


def step_kernel(last, extent, full, state, *refs):
    place = (state[2, 0:1, :], state[2, 1:2, :], *extent)
    count = state[2, 2, 0].astype(jnp.int32)
    if last:
        fractions, scale, scaled, final_velocity, displacement, potential_out = refs[:6]
    else:
        fractions_out, state_out, scale, scaled = refs[:4]
    pair_blocks, spread_blocks, own_columns, sums, density = refs[-5:]
    density[...] = jnp.zeros(density.shape, jnp.float32)
    spread_blocks[...] = jnp.zeros(spread_blocks.shape, jnp.float32)
    sums[...] = jnp.zeros(sums.shape, jnp.float32)

    def block_of(column, index, lanes):
        block = full[column, index, :, lanes]
        if last:
            moved = fractions[column, index // 2, index % 2, :, lanes]
            return jnp.concatenate([block[0:3], moved[0:3], block[6:8]], 0)
        return block

    row_index = iota((8, LANES), 0)
    pair_count = jnp.int32(0)
    spread_counts = []
    for column in range(5):
        spread_count = jnp.int32(0)
        for side in range(3):
            shift = jnp.where(
                row_index == 0,
                4.0 * (column - 2),
                jnp.where(row_index == 1, 16.0 * (side - 1), 0.0),
            )
            for part in range(4):
                lanes = pl.ds((part % 2) * LANES, LANES)
                block = block_of(column, side * 2 + part // 2, lanes) + shift
                alive = block[6, 0] > 0.0
                spread_blocks[column, spread_count] = block
                spread_count = spread_count + alive.astype(jnp.int32)
                if column in (1, 2, 3):
                    pair_blocks[pair_count, 0:3, :] = KAPPA * (block[0:3] + block[3:6])
                    pair_blocks[pair_count, 3:4, :] = -block[6:7]
                    pair_blocks[pair_count, 4:5, :] = block[7:8]
                    pair_count = pair_count + alive.astype(jnp.int32)
        spread_counts.append(spread_count)
    pair_blocks[pair_count] = jnp.zeros((8, LANES), jnp.float32)

    own_halves = []
    for half in range(2):
        own = jnp.concatenate([block_of(2, 2 + half, pl.ds(i * LANES, LANES)) for i in range(2)], 1)
        own_halves.append(own)
        packed = jnp.concatenate(
            [KAPPA * (own[0:3] + own[3:6]), own[7:8], jnp.zeros((4, 256), jnp.float32)], 0
        )
        turned = jnp.transpose(packed)
        rows = pl.ds(half * 256, 256)
        for row in range(3):
            own_columns[row, rows, :] = jnp.broadcast_to(turned[:, row : row + 1], (256, LANES))
        own_columns[3, rows, :] = jnp.broadcast_to(-turned[:, 3:4], (256, LANES))

    def add_rows(index, carry):
        rows = pl.ds(index * I_ROWS, I_ROWS)
        own_x, own_y, own_z, own_s = (own_columns[row, rows, :] for row in range(4))

        def add_blocks(step, totals):
            for part in range(2):
                block = pair_blocks[step * 2 + part]
                x = own_x - block[0:1]
                y = own_y - block[1:2]
                z = own_z - block[2:3]
                spread = own_s - block[4:5]
                inverse = 1.0 / spread
                factor = jnp.exp2((x * x + y * y + z * z) * inverse)
                factor = (factor * block[3:4]) * inverse
                totals = (totals[0] + factor * x, totals[1] + factor * y, totals[2] + factor * z)
            return totals

        zero = jnp.zeros((I_ROWS, LANES), jnp.float32)
        totals = lax.fori_loop(0, (pair_count + 1) // 2, add_blocks, (zero, zero, zero))
        for axis in range(3):
            sums[axis, rows, :] = totals[axis]
        return carry

    lax.fori_loop(0, (count + I_ROWS - 1) // I_ROWS, add_rows, 0)

    depth = iota((256, 256), 0).astype(jnp.float32)
    height = iota((32, 256), 0).astype(jnp.float32) - 8.0
    rows = rows_inside(place, -8, 32)

    def add_chunk(step, column, planes):
        chunk = jnp.concatenate(
            [spread_blocks[column, step * 2], spread_blocks[column, step * 2 + 1]], 1
        )
        fx, fy, fz = chunk[3:4], chunk[4:5], chunk[5:6]
        charge = chunk[6:7]
        selected = jnp.where(depth == chunk[2:3], 1.0, 0.0).astype(jnp.bfloat16)
        weight_y = jnp.where(
            height == chunk[1:2], 1.0 - fy, jnp.where(height == chunk[1:2] + 1.0, fy, 0.0)
        )
        weight_y = jnp.where(rows, weight_y, 0.0)
        weights = []
        for amount in (charge * (1.0 - fz), charge * fz):
            for plane in planes:
                weight_x = jnp.where(
                    chunk[0:1] == plane, 1.0 - fx, jnp.where(chunk[0:1] + 1.0 == plane, fx, 0.0)
                )
                weights.append((weight_x * amount * plane_inside(place, plane)) * weight_y)
        added = dot_exact(jnp.concatenate(weights, 0), selected, ((1,), (1,)))
        return added.reshape(2, len(planes), 32, 256)

    def add_chunks(step, carry):
        added = [
            add_chunk(step, column, planes)
            for column, planes in enumerate(
                ((-4,), range(-4, 1), range(0, 5), range(4, 9), (8,))
            )
        ]
        for part in range(2):
            far_left, left, own, right, far_right = (added[column][part] for column in range(5))
            pieces = (
                far_left + left[0:1],
                left[1:4],
                left[4:5] + own[0:1],
                own[1:4],
                own[4:5] + right[0:1],
                right[1:4],
                right[4:5] + far_right,
            )
            start = 0
            for piece in pieces:
                where = pl.ds(start, piece.shape[0])
                density[part, where] = density[part, where] + piece
                start += piece.shape[0]
        return carry

    longest = functools.reduce(jnp.maximum, spread_counts)
    lax.fori_loop(0, (longest + 1) // 2, add_chunks, 0)

    if not last:
        inverse_scale(place, full, scale, scaled)
    matrix = band(BLUR)
    value = [planes_filtered(density[part], BLUR, 9) for part in range(2)]
    value = value[0] + pltpu.roll(value[1], 1, 2)
    value = depth_filtered(rows_filtered(value, BLUR), matrix, 2)
    residual = value * scale[...] - scaled[...]
    value = rows_filtered(planes_filtered(residual, BLUR, 5), BLUR)
    potential = depth_filtered(value, matrix, 2)
    if last:
        potential_out[...] = potential[0:4, 8:24]

    field = potential[:, 8:32].reshape(120, 256)
    both = jnp.concatenate([field, pltpu.roll(field, 255, 1)], 0)
    ones = jnp.ones((8, LANES), jnp.bfloat16)
    height = iota((24, 256), 0).astype(jnp.float32)
    rows = rows_inside(place, 0, 24)
    edge = plane_inside(place, 4)
    for half in range(2):
        own = own_halves[half]
        gx, gy, gz, fx, fy, fz = (own[row : row + 1] for row in range(6))
        selected = jnp.where(depth == gz, 1.0, 0.0).astype(jnp.bfloat16)
        taken = dot_exact(both, selected, ((1,), (0,))).reshape(2, 5, 24, 256)
        lower, upper = (height == gy) & rows, (height == gy + 1.0) & rows
        weight_y = jnp.where(lower, 1.0 - fy, jnp.where(upper, fy, 0.0))
        slope_y = jnp.where(lower, -1.0, jnp.where(upper, 1.0, 0.0))
        mixed = [jnp.zeros((24, 256), jnp.float32) for _ in range(3)]
        for plane in range(5):
            slope_z = taken[1, plane] - taken[0, plane]
            product = taken[0, plane] + fz * slope_z
            lower, upper = gx == plane, gx + 1.0 == plane
            weight_x = jnp.where(lower, 1.0 - fx, jnp.where(upper, fx, 0.0))
            slope_x = jnp.where(lower, -1.0, jnp.where(upper, 1.0, 0.0))
            if plane == 4:
                weight_x, slope_x = weight_x * edge, slope_x * edge
            mixed[0] = mixed[0] + slope_x * product
            mixed[1] = mixed[1] + weight_x * product
            mixed[2] = mixed[2] + weight_x * slope_z
        gradient = (
            jnp.sum(mixed[0] * weight_y, 0, keepdims=True),
            jnp.sum(mixed[1] * slope_y, 0, keepdims=True),
            jnp.sum(mixed[2] * weight_y, 0, keepdims=True),
        )
        charge = own[6:7]
        values = state[half]
        mass, live = values[6:7], values[7:8]
        if not last:
            state_out[half, 6:8, :] = values[6:8]
            state_out[2] = state[2]
            fractions_out[half, 3:4, :] = jnp.zeros((1, 256), jnp.float32)
        for axis in range(3):
            parts = split(sums[axis, pl.ds(half * 256, 256), :], 2)
            pair = dot(ones, parts[0], ((1,), (1,))) + dot(ones, parts[1], ((1,), (1,)))
            force = charge * (pair[0:1] * (1.0 / KAPPA) - gradient[axis])
            velocity = values[axis : axis + 1] + TIME_STEP * force / mass
            moved = values[axis + 3 : axis + 4] + TIME_STEP * velocity
            if last:
                lanes = pl.ds(half * 256, 256)
                final_velocity[axis, 0, :, lanes] = velocity * live
                displacement[axis, 0, :, lanes] = moved * live
            else:
                state_out[half, axis : axis + 1, :] = velocity
                state_out[half, axis + 3 : axis + 4, :] = moved
                fractions_out[half, axis : axis + 1, :] = (
                    own[axis + 3 : axis + 4] + TIME_STEP * velocity
                )


SMEM = pl.BlockSpec(memory_space=pltpu.SMEM)
VMEM = pl.BlockSpec(memory_space=pltpu.VMEM)


def shape(*dims):
    return jax.ShapeDtypeStruct(dims, jnp.float32)


def links():
    chips = lax.axis_size("cells") // 2
    groups = lax.axis_size("grp")

    def coloured(count, first):
        pairs = []
        for left in range(first, count - 1, 2):
            pairs += [(left, left + 1), (left + 1, left)]
        return pairs

    def doubled(pairs):
        return [(2 * a + core, 2 * b + core) for a, b in pairs for core in range(2)]

    return {
        "odd": ("cells", doubled(coloured(chips, 1))),
        "even": ("cells", doubled(coloured(chips, 0))),
        "rows_even": ("grp", coloured(groups, 0)),
        "rows_odd": ("grp", coloured(groups, 1)),
        "pair": ("cells", [(i, i ^ 1) for i in range(2 * chips)]),
    }


def spread_out(own, rows, groups, flags):
    even_chip, even_row, _ = flags

    def send(value, link):
        return lax.ppermute(value, *groups[link])

    odd = send(own, "odd")
    even = send(own, "even")
    left = jnp.where(even_chip, odd, even)
    right = jnp.where(even_chip, even, odd)
    columns = jnp.stack([own, left, right])
    from_even = send(rows(columns, even_row), "rows_even")
    from_odd = send(rows(columns, ~even_row), "rows_odd")
    above = jnp.where(even_row, from_even, from_odd)
    below = jnp.where(even_row, from_odd, from_even)
    return columns, below, above, functools.partial(send, link="pair")


def finish(full, send, first_core):
    chosen = jnp.where(first_core, full[2], full[1])
    got = send(jnp.stack([full[0], chosen]))
    minus = jnp.where(first_core, got[1], got[0])
    plus = jnp.where(first_core, got[0], got[1])
    return jnp.stack([full[1], minus, full[0], plus, full[2]])


def per_device(fraction, velocity, anchor, atom_types, counts, type_table, target):
    cells, groups_count = lax.axis_size("cells"), lax.axis_size("grp")
    cell, group = lax.axis_index("cells"), lax.axis_index("grp")
    groups = links()
    flags = ((cell // 2) % 2 == 0, group % 2 == 0, cell % 2 == 0)
    extent = (4.0 * cells, 16.0 * groups_count)

    own, state = pl.pallas_call(
        prep_kernel,
        out_shape=(shape(10, 8, 256), shape(3, 8, 256)),
        in_specs=[SMEM, SMEM, VMEM, VMEM, VMEM, VMEM, VMEM],
        out_specs=(VMEM, VMEM),
        name="prep",
    )(counts, type_table, fraction, velocity, anchor, atom_types, target)

    state = state + jnp.where(cell < 0, 1.0, 0.0)

    def rows_first(columns, upper):
        fields = columns[:, 2:].reshape(3, 4, 2, 8, 256)
        return jnp.concatenate(
            [columns[:, :2], jnp.where(upper, fields[:, :, 1], fields[:, :, 0])], 1
        )

    columns, below, above, send = spread_out(own, rows_first, groups, flags)
    full = jnp.concatenate(
        [
            jnp.stack([below[:, :2], columns[:, :2], above[:, :2]], 1).reshape(3, 6, 8, 256),
            jnp.concatenate(
                [
                    below[:, 2:, None],
                    columns[:, 2:].reshape(3, 4, 2, 8, 256),
                    above[:, 2:, None],
                ],
                2,
            ).reshape(3, 16, 8, 256),
        ],
        1,
    )
    full = finish(full, send, flags[2])

    field = shape(9, 32, 256)
    scratch = [
        pltpu.VMEM((38, 8, LANES), jnp.float32),
        pltpu.VMEM((5, 14, 8, LANES), jnp.float32),
        pltpu.VMEM((4, 512, LANES), jnp.float32),
        pltpu.VMEM((3, 512, LANES), jnp.float32),
        pltpu.VMEM((2, 13, 32, 256), jnp.float32),
    ]
    fractions, state, scale, scaled = pl.pallas_call(
        functools.partial(step_kernel, False, extent),
        out_shape=(shape(2, 4, 256), shape(3, 8, 256), field, field),
        in_specs=[VMEM, VMEM],
        out_specs=(VMEM,) * 4,
        scratch_shapes=scratch,
        name="step",
        compiler_params=pltpu.CompilerParams(vmem_limit_bytes=24 << 20),
    )(full, state)

    columns, below, above, send = spread_out(fractions, lambda c, upper: c, groups, flags)
    moved = finish(jnp.stack([below, columns, above], 1), send, flags[2])
    return pl.pallas_call(
        functools.partial(step_kernel, True, extent),
        out_shape=(shape(*velocity.shape), shape(*velocity.shape), shape(*target.shape)),
        in_specs=[VMEM] * 5,
        out_specs=(VMEM,) * 3,
        scratch_shapes=scratch,
        name="step_last",
        compiler_params=pltpu.CompilerParams(vmem_limit_bytes=24 << 20),
    )(full, state, moved, scale, scaled)


def solution(mesh):
    placed = (
        P(None, "cells", "grp", None),
        P(None, "cells", "grp", None),
        P(None, "cells", "grp", None),
        P("cells", "grp", None),
        P("cells", "grp"),
        P(),
        P("cells", "grp", None),
    )
    return jax.shard_map(
        per_device,
        mesh=mesh,
        in_specs=placed,
        out_specs=(
            P(None, "cells", "grp", None),
            P(None, "cells", "grp", None),
            P("cells", "grp", None),
        ),
        check_vma=False,
    )
```

```python
import functools

import jax
import jax.numpy as jnp
from jax import lax
from jax.experimental import pallas as pl
from jax.experimental.pallas import tpu as pltpu
from jax.sharding import PartitionSpec as P


EPSILON = 1e-06
TIME_STEP = 0.5
BLUR = tuple(tap / 4096.0 for tap in (1.0, 4.0, 6.0, 4.0, 1.0))
KAPPA = 0.8493218002880191
LANES = 128
I_ROWS = 64


def dot(a, b, dims, precision=None):
    return lax.dot_general(
        a, b, (dims, ((), ())), precision=precision, preferred_element_type=jnp.float32
    )


def split(value, pieces):
    parts = []
    for _ in range(pieces):
        parts.append(value.astype(jnp.bfloat16))
        value = value - parts[-1].astype(jnp.float32)
    return parts


def dot_exact(a, b, dims, pieces=2):
    count = a.shape[0]
    product = dot(jnp.concatenate(split(a, pieces), 0), b, dims)
    total = product[count * (pieces - 1) :]
    for piece in reversed(range(pieces - 1)):
        total = total + product[count * piece : count * (piece + 1)]
    return total


def iota(shape, dim):
    return lax.broadcasted_iota(jnp.int32, shape, dim)


def band(weights):
    radius = (len(weights) - 1) // 2
    offset = iota((256, 256), 0) - iota((256, 256), 1)
    result = jnp.zeros((256, 256), jnp.float32)
    for shift in range(-radius, radius + 1):
        result = jnp.where(offset == shift, weights[shift + radius], result)
    return result.astype(jnp.bfloat16)


def rows_blurred(values):
    size = values.shape[1]
    near = pltpu.roll(values, 1, 1) + pltpu.roll(values, size - 1, 1)
    far = pltpu.roll(values, 2, 1) + pltpu.roll(values, size - 2, 1)
    return 6.0 * values + 4.0 * near + far


def rows_boxed(values):
    pairs = values + pltpu.roll(values, 1, 1)
    fours = pairs + pltpu.roll(pairs, 2, 1)
    eights = fours + pltpu.roll(fours, 4, 1)
    nines = eights + pltpu.roll(values, 8, 1)
    return pltpu.roll(nines, values.shape[1] - 4, 1)


def depth_filtered(values, matrix, pieces):
    flat = values.reshape(values.shape[0] * 32, 256)
    return dot_exact(flat, matrix, ((1,), (0,)), pieces).reshape(values.shape)


def planes_blurred(values, count):
    near = values[1 : 1 + count] + values[3 : 3 + count]
    far = values[0:count] + values[4 : 4 + count]
    return 6.0 * values[2 : 2 + count] + 4.0 * near + far


def plane_inside(place, plane):
    position = place[0] * 4.0 + plane
    return ((position >= 0.0) & (position < place[2])).astype(jnp.float32)


def rows_inside(place, first, rows):
    position = place[1] * 16.0 + first + iota((rows, 256), 0).astype(jnp.float32)
    return (position >= 0.0) & (position < place[3])


def prep_kernel(counts, table, fraction, velocity, anchor, kinds, target, sent, state):
    info = (lax.axis_index("cells"), lax.axis_index("grp"), counts[0, 0])
    for row, value in enumerate(info):
        state[2, row : row + 1, :] = jnp.full((1, 256), value, jnp.int32).astype(jnp.float32)
    state[2, 3:8, :] = jnp.zeros((5, 256), jnp.float32)
    for half in range(2):
        lanes = pl.ds(half * 256, 256)
        kind = kinds[0, :, lanes]
        live = (iota((1, 256), 1) + half * 256 < counts[0, 0]).astype(jnp.float32)
        values = []
        for row in range(3):
            value = jnp.zeros((1, 256), jnp.float32)
            for option in range(table.shape[1]):
                value = jnp.where(kind == option, table[row, option], value)
            values.append(value)
        for row in range(3):
            sent[half, row : row + 1, :] = anchor[row, 0, :, lanes].astype(jnp.float32)
            sent[half, row + 3 : row + 4, :] = fraction[row, 0, :, lanes]
            state[half, row : row + 1, :] = velocity[row, 0, :, lanes]
            state[half, row + 3 : row + 4, :] = jnp.zeros((1, 256), jnp.float32)
        sent[half, 6:7, :] = values[0] * live
        sent[half, 7:8, :] = values[1] * values[1]
        state[half, 6:7, :] = values[2]
        state[half, 7:8, :] = live
    for plane in range(4):
        for half in range(2):
            sent[2 + 2 * plane + half] = target[plane, pl.ds(8 * half, 8), :]


def inverse_scale(place, full, scale, scaled):
    matrix = band((1.0,) * 9)
    rows = rows_inside(place, -8, 32)
    planes = [full[index // 4, pl.ds(6 + index % 4 * 4, 4)] for index in range(2, 19)]
    planes = jnp.stack([plane.reshape(32, 256) for plane in planes])
    sums = []
    for source in (planes, planes * planes):
        pairs = source[0:16] + source[1:17]
        fours = pairs[0:14] + pairs[2:16]
        summed = fours[0:9] + fours[4:13] + source[8:17]
        sums.append(depth_filtered(rows_boxed(summed), matrix, 3) * (1.0 / 729.0))
    value = lax.rsqrt(sums[1] - sums[0] * sums[0] + EPSILON)
    for plane in range(9):
        kept = jnp.where(rows, value[plane], 0.0) * plane_inside(place, plane - 2)
        scale[plane] = kept
        scaled[plane] = kept * planes[plane + 4]


def place_of(state, extent):
    return (state[2, 0:1, :], state[2, 1:2, :], *extent)


def add_pair_block(block, pair_blocks, count):
    pair_blocks[count, 0:3, :] = KAPPA * (block[0:3] + block[3:6])
    pair_blocks[count, 3:4, :] = -block[6:7]
    pair_blocks[count, 4:5, :] = block[7:8]
    return count + (block[6, 0] > 0.0).astype(jnp.int32)


def pair_sums(state, pair_blocks, pair_count, own_columns, sums_in, sums_out):
    pair_blocks[pair_count] = jnp.zeros((8, LANES), jnp.float32)
    count = state[2, 2, 0].astype(jnp.int32)

    def add_rows(index, carry):
        rows = pl.ds(index * I_ROWS, I_ROWS)
        own_x, own_y, own_z, own_s = (own_columns[row, rows, :] for row in range(4))

        def add_blocks(step, totals):
            for part in range(2):
                block = pair_blocks[step * 2 + part]
                x = own_x - block[0:1]
                y = own_y - block[1:2]
                z = own_z - block[2:3]
                spread = own_s - block[4:5]
                inverse = 1.0 / spread
                factor = jnp.exp2((x * x + y * y + z * z) * inverse)
                factor = (factor * block[3:4]) * inverse
                totals = (totals[0] + factor * x, totals[1] + factor * y, totals[2] + factor * z)
            return totals

        if sums_in is None:
            totals = (jnp.zeros((I_ROWS, LANES), jnp.float32),) * 3
        else:
            totals = tuple(sums_in[axis, rows, :] for axis in range(3))
        totals = lax.fori_loop(0, (pair_count + 1) // 2, add_blocks, totals)
        for axis in range(3):
            sums_out[axis, rows, :] = totals[axis]
        return carry

    lax.fori_loop(0, (count + I_ROWS - 1) // I_ROWS, add_rows, 0)


def chunk_density(chunk, planes, place):
    depth = iota((256, 256), 0).astype(jnp.float32)
    height = iota((32, 256), 0).astype(jnp.float32) - 8.0
    fx, fy, fz = chunk[3:4], chunk[4:5], chunk[5:6]
    charge = chunk[6:7]
    selected = jnp.where(depth == chunk[2:3], 1.0, 0.0).astype(jnp.bfloat16)
    weight_y = jnp.where(
        height == chunk[1:2], 1.0 - fy, jnp.where(height == chunk[1:2] + 1.0, fy, 0.0)
    )
    weight_y = jnp.where(rows_inside(place, -8, 32), weight_y, 0.0)
    weights = []
    for amount in (charge * (1.0 - fz), charge * fz):
        for plane in planes:
            weight_x = jnp.where(
                chunk[0:1] == plane, 1.0 - fx, jnp.where(chunk[0:1] + 1.0 == plane, fx, 0.0)
            )
            weights.append((weight_x * amount * plane_inside(place, plane)) * weight_y)
    added = dot_exact(jnp.concatenate(weights, 0), selected, ((1,), (1,)))
    return added.reshape(2, len(planes), 32, 256)


def joined(block, moved):
    return jnp.concatenate([block[0:3], moved[0:3], block[6:8]], 0)


def own_kernel(moving, extent, sent, state, *refs):
    if moving:
        fractions, own_columns, sums, spread, pair_blocks = refs
    else:
        staged, own_columns, sums, spread, pair_blocks = refs
        staged[...] = state[...]
    place = place_of(state, extent)
    pair_count = jnp.int32(0)
    spread[...] = jnp.zeros(spread.shape, jnp.float32)
    for half in range(2):
        own = joined(sent[half], fractions[half]) if moving else sent[half]
        packed = jnp.concatenate(
            [KAPPA * (own[0:3] + own[3:6]), own[7:8], jnp.zeros((4, 256), jnp.float32)], 0
        )
        turned = jnp.transpose(packed)
        rows = pl.ds(half * 256, 256)
        for row in range(3):
            own_columns[row, rows, :] = jnp.broadcast_to(turned[:, row : row + 1], (256, LANES))
        own_columns[3, rows, :] = jnp.broadcast_to(-turned[:, 3:4], (256, LANES))
        for part in range(2):
            block = own[:, part * LANES : (part + 1) * LANES]
            pair_count = add_pair_block(block, pair_blocks, pair_count)

        @pl.when(own[6, 0] > 0.0)
        def _(own=own):
            spread[...] += chunk_density(own, range(5), place)

    pair_sums(state, pair_blocks, pair_count, own_columns, None, sums)


def column_kernel(moving, full, state, *refs):
    if moving:
        fractions, own_columns, sums_in, sums, pair_blocks = refs
    else:
        own_columns, sums_in, sums, pair_blocks = refs
    pair_count = jnp.int32(0)
    row_index = iota((8, LANES), 0)
    for side in (0, 2):
        shift = jnp.where(row_index == 1, 16.0 * (side - 1), 0.0)
        for part in range(4):
            lanes = pl.ds((part % 2) * LANES, LANES)
            block = full[0, side * 2 + part // 2, :, lanes]
            if moving:
                block = joined(block, fractions[0, side, part // 2, :, lanes])
            pair_count = add_pair_block(block + shift, pair_blocks, pair_count)
    pair_sums(state, pair_blocks, pair_count, own_columns, sums_in, sums)


def step_kernel(last, extent, full, state, own_columns, sums_in, spread, *refs):
    place = place_of(state, extent)
    if last:
        fractions, scale, scaled, final_velocity, displacement, potential_out = refs[:6]
    else:
        fractions_out, state_out, scale, scaled = refs[:4]
    pair_blocks, spread_blocks, sums, density = refs[-4:]
    for part in range(2):
        density[part, 0:4] = jnp.zeros((4, 32, 256), jnp.float32)
        density[part, 4:9] = spread[part]
        density[part, 9:13] = jnp.zeros((4, 32, 256), jnp.float32)
    spread_blocks[...] = jnp.zeros(spread_blocks.shape, jnp.float32)

    def block_of(column, index, lanes):
        block = full[column, index, :, lanes]
        if last:
            return joined(block, fractions[column, index // 2, index % 2, :, lanes])
        return block

    row_index = iota((8, LANES), 0)
    pair_count = jnp.int32(0)
    spread_counts = []
    for column in range(5):
        spread_count = jnp.int32(0)
        for side in range(3):
            if (column, side) == (2, 1):
                continue
            shift = jnp.where(
                row_index == 0,
                4.0 * (column - 2),
                jnp.where(row_index == 1, 16.0 * (side - 1), 0.0),
            )
            for part in range(4):
                lanes = pl.ds((part % 2) * LANES, LANES)
                block = block_of(column, side * 2 + part // 2, lanes) + shift
                spread_blocks[column, spread_count] = block
                spread_count = spread_count + (block[6, 0] > 0.0).astype(jnp.int32)
                if column in (1, 3):
                    pair_count = add_pair_block(block, pair_blocks, pair_count)
        spread_counts.append(spread_count)
    pair_sums(state, pair_blocks, pair_count, own_columns, sums_in, sums)

    def add_chunks(step, carry):
        added = []
        for column, planes in enumerate(
            ((-4,), range(-4, 1), range(0, 5), range(4, 9), (8,))
        ):
            chunk = jnp.concatenate(
                [spread_blocks[column, step * 2], spread_blocks[column, step * 2 + 1]], 1
            )
            added.append(chunk_density(chunk, planes, place))
        for part in range(2):
            far_left, left, own, right, far_right = (added[column][part] for column in range(5))
            pieces = (
                far_left + left[0:1],
                left[1:4],
                left[4:5] + own[0:1],
                own[1:4],
                own[4:5] + right[0:1],
                right[1:4],
                right[4:5] + far_right,
            )
            start = 0
            for piece in pieces:
                where = pl.ds(start, piece.shape[0])
                density[part, where] = density[part, where] + piece
                start += piece.shape[0]
        return carry

    longest = functools.reduce(jnp.maximum, spread_counts)
    lax.fori_loop(0, (longest + 1) // 2, add_chunks, 0)

    if not last:
        inverse_scale(place, full, scale, scaled)
    matrix = band(BLUR)
    value = density[0] + pltpu.roll(density[1], 1, 2)
    value = depth_filtered(rows_blurred(planes_blurred(value, 9)), matrix, 2)
    residual = value * scale[...] - scaled[...]
    potential = depth_filtered(rows_blurred(planes_blurred(residual, 5)), matrix, 2)
    if last:
        potential_out[...] = potential[0:4, 8:24]

    field = potential[:, 8:32].reshape(120, 256)
    both = jnp.concatenate([field, pltpu.roll(field, 255, 1)], 0)
    ones = jnp.ones((8, LANES), jnp.bfloat16)
    depth = iota((256, 256), 0).astype(jnp.float32)
    height = iota((24, 256), 0).astype(jnp.float32)
    rows = rows_inside(place, 0, 24)
    edge = plane_inside(place, 4)
    for half in range(2):
        own = jnp.concatenate([block_of(2, 2 + half, pl.ds(i * LANES, LANES)) for i in range(2)], 1)
        gx, gy, gz, fx, fy, fz = (own[row : row + 1] for row in range(6))
        selected = jnp.where(depth == gz, 1.0, 0.0).astype(jnp.bfloat16)
        taken = dot_exact(both, selected, ((1,), (0,))).reshape(2, 5, 24, 256)
        lower, upper = (height == gy) & rows, (height == gy + 1.0) & rows
        weight_y = jnp.where(lower, 1.0 - fy, jnp.where(upper, fy, 0.0))
        slope_y = jnp.where(lower, -1.0, jnp.where(upper, 1.0, 0.0))
        mixed = [jnp.zeros((24, 256), jnp.float32) for _ in range(3)]
        for plane in range(5):
            slope_z = taken[1, plane] - taken[0, plane]
            product = taken[0, plane] + fz * slope_z
            lower, upper = gx == plane, gx + 1.0 == plane
            weight_x = jnp.where(lower, 1.0 - fx, jnp.where(upper, fx, 0.0))
            slope_x = jnp.where(lower, -1.0, jnp.where(upper, 1.0, 0.0))
            if plane == 4:
                weight_x, slope_x = weight_x * edge, slope_x * edge
            mixed[0] = mixed[0] + slope_x * product
            mixed[1] = mixed[1] + weight_x * product
            mixed[2] = mixed[2] + weight_x * slope_z
        gradient = (
            jnp.sum(mixed[0] * weight_y, 0, keepdims=True),
            jnp.sum(mixed[1] * slope_y, 0, keepdims=True),
            jnp.sum(mixed[2] * weight_y, 0, keepdims=True),
        )
        charge = own[6:7]
        values = state[half]
        mass, live = values[6:7], values[7:8]
        if not last:
            state_out[half, 6:8, :] = values[6:8]
            state_out[2] = state[2]
            fractions_out[half, 3:4, :] = jnp.zeros((1, 256), jnp.float32)
        for axis in range(3):
            parts = split(sums[axis, pl.ds(half * 256, 256), :], 2)
            pair = dot(ones, parts[0], ((1,), (1,))) + dot(ones, parts[1], ((1,), (1,)))
            force = charge * (pair[0:1] * (1.0 / KAPPA) - gradient[axis])
            force = jnp.where(charge > 0.0, force, 0.0)
            velocity = values[axis : axis + 1] + TIME_STEP * force / mass
            moved = values[axis + 3 : axis + 4] + TIME_STEP * velocity
            if last:
                lanes = pl.ds(half * 256, 256)
                final_velocity[axis, 0, :, lanes] = velocity * live
                displacement[axis, 0, :, lanes] = moved * live
            else:
                state_out[half, axis : axis + 1, :] = velocity
                state_out[half, axis + 3 : axis + 4, :] = moved
                fractions_out[half, axis : axis + 1, :] = (
                    own[axis + 3 : axis + 4] + TIME_STEP * velocity
                )


SMEM = pl.BlockSpec(memory_space=pltpu.SMEM)
VMEM = pl.BlockSpec(memory_space=pltpu.VMEM)


def shape(*dims):
    return jax.ShapeDtypeStruct(dims, jnp.float32)


def links():
    chips = lax.axis_size("cells") // 2
    groups = lax.axis_size("grp")

    def coloured(count, first):
        pairs = []
        for left in range(first, count - 1, 2):
            pairs += [(left, left + 1), (left + 1, left)]
        return pairs

    def doubled(pairs):
        return [(2 * a + core, 2 * b + core) for a, b in pairs for core in range(2)]

    return {
        "odd": ("cells", doubled(coloured(chips, 1))),
        "even": ("cells", doubled(coloured(chips, 0))),
        "rows_even": ("grp", coloured(groups, 0)),
        "rows_odd": ("grp", coloured(groups, 1)),
        "pair": ("cells", [(i, i ^ 1) for i in range(2 * chips)]),
    }


def spread_out(own, rows, groups, flags):
    even_chip, even_row, _ = flags

    def send(value, link):
        return lax.ppermute(value, *groups[link])

    odd = send(own, "odd")
    even = send(own, "even")
    left = jnp.where(even_chip, odd, even)
    right = jnp.where(even_chip, even, odd)
    columns = jnp.stack([own, left, right])
    from_even = send(rows(columns, even_row), "rows_even")
    from_odd = send(rows(columns, ~even_row), "rows_odd")
    above = jnp.where(even_row, from_even, from_odd)
    below = jnp.where(even_row, from_odd, from_even)

    def send_partner(value):
        return send(value, "pair")

    return columns, below, above, send_partner


def finish(full, send, first_core):
    chosen = jnp.where(first_core, full[2], full[1])
    got = send(jnp.stack([full[0], chosen]))
    minus = jnp.where(first_core, got[1], got[0])
    plus = jnp.where(first_core, got[0], got[1])
    return jnp.stack([full[1], minus, full[0], plus, full[2]])


def per_device(fraction, velocity, anchor, atom_types, counts, type_table, target):
    cells, groups_count = lax.axis_size("cells"), lax.axis_size("grp")
    cell, group = lax.axis_index("cells"), lax.axis_index("grp")
    groups = links()
    flags = ((cell // 2) % 2 == 0, group % 2 == 0, cell % 2 == 0)
    extent = (4.0 * cells, 16.0 * groups_count)

    own, state = pl.pallas_call(
        prep_kernel,
        out_shape=(shape(10, 8, 256), shape(3, 8, 256)),
        in_specs=[SMEM, SMEM, VMEM, VMEM, VMEM, VMEM, VMEM],
        out_specs=(VMEM, VMEM),
        name="prep",
    )(counts, type_table, fraction, velocity, anchor, atom_types, target)

    table = shape(4, 512, LANES)
    totals = shape(3, 512, LANES)
    spread = shape(2, 5, 32, 256)
    limit = pltpu.CompilerParams(vmem_limit_bytes=24 << 20)

    def alone(turn, *operands):
        outs = (table, totals, spread)
        if turn == 0:
            outs = (shape(3, 8, 256),) + outs
        return pl.pallas_call(
            functools.partial(own_kernel, turn > 0, extent),
            out_shape=outs,
            in_specs=[VMEM] * len(operands),
            out_specs=(VMEM,) * len(outs),
            scratch_shapes=[pltpu.VMEM((6, 8, LANES), jnp.float32)],
            name="alone",
            compiler_params=limit,
        )(*operands)

    def beside(turn, *operands):
        return pl.pallas_call(
            functools.partial(column_kernel, turn > 0),
            out_shape=totals,
            in_specs=[VMEM] * len(operands),
            out_specs=VMEM,
            scratch_shapes=[pltpu.VMEM((10, 8, LANES), jnp.float32)],
            name="beside",
            compiler_params=limit,
        )(*operands)

    state, own_columns, sums, own_spread = alone(0, own, state)

    def rows_first(columns, upper):
        fields = columns[:, 2:].reshape(3, 4, 2, 8, 256)
        return jnp.concatenate(
            [columns[:, :2], jnp.where(upper, fields[:, :, 1], fields[:, :, 0])], 1
        )

    columns, below, above, send = spread_out(own, rows_first, groups, flags)
    full = jnp.concatenate(
        [
            jnp.stack([below[:, :2], columns[:, :2], above[:, :2]], 1).reshape(3, 6, 8, 256),
            jnp.concatenate(
                [
                    below[:, 2:, None],
                    columns[:, 2:].reshape(3, 4, 2, 8, 256),
                    above[:, 2:, None],
                ],
                2,
            ).reshape(3, 16, 8, 256),
        ],
        1,
    )
    column = full
    sums = beside(0, column, state, own_columns, sums)
    full = finish(full, send, flags[2])

    field = shape(9, 32, 256)
    scratch = [
        pltpu.VMEM((26, 8, LANES), jnp.float32),
        pltpu.VMEM((5, 14, 8, LANES), jnp.float32),
        pltpu.VMEM((3, 512, LANES), jnp.float32),
        pltpu.VMEM((2, 13, 32, 256), jnp.float32),
    ]
    fractions, state, scale, scaled = pl.pallas_call(
        functools.partial(step_kernel, False, extent),
        out_shape=(shape(2, 4, 256), shape(3, 8, 256), field, field),
        in_specs=[VMEM] * 5,
        out_specs=(VMEM,) * 4,
        scratch_shapes=scratch,
        name="step",
        compiler_params=pltpu.CompilerParams(vmem_limit_bytes=24 << 20),
    )(full, state, own_columns, sums, own_spread)

    own_columns, sums, own_spread = alone(1, own, state, fractions)

    columns, below, above, send = spread_out(fractions, lambda c, upper: c, groups, flags)
    moved = jnp.stack([below, columns, above], 1)
    sums = beside(1, column, state, moved, own_columns, sums)
    moved = finish(moved, send, flags[2])
    return pl.pallas_call(
        functools.partial(step_kernel, True, extent),
        out_shape=(shape(*velocity.shape), shape(*velocity.shape), shape(*target.shape)),
        in_specs=[VMEM] * 8,
        out_specs=(VMEM,) * 3,
        scratch_shapes=scratch,
        name="step_last",
        compiler_params=pltpu.CompilerParams(vmem_limit_bytes=24 << 20),
    )(full, state, own_columns, sums, own_spread, moved, scale, scaled)


def solution(mesh):
    placed = (
        P(None, "cells", "grp", None),
        P(None, "cells", "grp", None),
        P(None, "cells", "grp", None),
        P("cells", "grp", None),
        P("cells", "grp"),
        P(),
        P("cells", "grp", None),
    )
    return jax.shard_map(
        per_device,
        mesh=mesh,
        in_specs=placed,
        out_specs=(
            P(None, "cells", "grp", None),
            P(None, "cells", "grp", None),
            P("cells", "grp", None),
        ),
        check_vma=False,
    )
```

```python
import functools

import jax
import jax.numpy as jnp
from jax import lax
from jax.experimental import pallas as pl
from jax.experimental.pallas import tpu as pltpu
from jax.sharding import PartitionSpec as P


EPSILON = 1e-06
TIME_STEP = 0.5
BLUR = tuple(tap / 4096.0 for tap in (1.0, 4.0, 6.0, 4.0, 1.0))
KAPPA = 0.8493218002880191
LANES = 128
I_ROWS = 64


def dot(a, b, dims, precision=None):
    return lax.dot_general(
        a, b, (dims, ((), ())), precision=precision, preferred_element_type=jnp.float32
    )


def split(value, pieces):
    parts = []
    for _ in range(pieces):
        parts.append(value.astype(jnp.bfloat16))
        value = value - parts[-1].astype(jnp.float32)
    return parts


def dot_exact(a, b, dims, pieces=2):
    count = a.shape[0]
    product = dot(jnp.concatenate(split(a, pieces), 0), b, dims)
    total = product[count * (pieces - 1) :]
    for piece in reversed(range(pieces - 1)):
        total = total + product[count * piece : count * (piece + 1)]
    return total


def iota(shape, dim):
    return lax.broadcasted_iota(jnp.int32, shape, dim)


def band(weights):
    radius = (len(weights) - 1) // 2
    offset = iota((256, 256), 0) - iota((256, 256), 1)
    result = jnp.zeros((256, 256), jnp.float32)
    for shift in range(-radius, radius + 1):
        result = jnp.where(offset == shift, weights[shift + radius], result)
    return result.astype(jnp.bfloat16)


def rows_blurred(values):
    size = values.shape[1]
    near = pltpu.roll(values, 1, 1) + pltpu.roll(values, size - 1, 1)
    far = pltpu.roll(values, 2, 1) + pltpu.roll(values, size - 2, 1)
    return 6.0 * values + 4.0 * near + far


def rows_boxed(values):
    pairs = values + pltpu.roll(values, 1, 1)
    fours = pairs + pltpu.roll(pairs, 2, 1)
    eights = fours + pltpu.roll(fours, 4, 1)
    nines = eights + pltpu.roll(values, 8, 1)
    return pltpu.roll(nines, values.shape[1] - 4, 1)


def depth_filtered(values, matrix, pieces):
    flat = values.reshape(values.shape[0] * 32, 256)
    return dot_exact(flat, matrix, ((1,), (0,)), pieces).reshape(values.shape)


def planes_blurred(values, count):
    near = values[1 : 1 + count] + values[3 : 3 + count]
    far = values[0:count] + values[4 : 4 + count]
    return 6.0 * values[2 : 2 + count] + 4.0 * near + far


def plane_inside(place, plane):
    position = place[0] * 4.0 + plane
    return ((position >= 0.0) & (position < place[2])).astype(jnp.float32)


def rows_inside(place, first, rows):
    position = place[1] * 16.0 + first + iota((rows, 256), 0).astype(jnp.float32)
    return (position >= 0.0) & (position < place[3])


def prep_kernel(counts, *refs):
    inputs, (sent, state), held, sems = refs[:6], refs[6:8], refs[8:14], refs[14]
    copies = [pltpu.make_async_copy(*pair, sems.at[i]) for i, pair in enumerate(zip(inputs, held))]
    for copy in copies:
        copy.start()
    table, fraction, velocity, anchor, kinds, target = held
    info = (lax.axis_index("cells"), lax.axis_index("grp"), counts[0, 0])
    for row, value in enumerate(info):
        state[2, row : row + 1, :] = jnp.full((1, 256), value, jnp.int32).astype(jnp.float32)
    state[2, 3:8, :] = jnp.zeros((5, 256), jnp.float32)
    for copy in copies:
        copy.wait()
    for half in range(2):
        lanes = pl.ds(half * 256, 256)
        kind = kinds[0, :, lanes]
        live = (iota((1, 256), 1) + half * 256 < counts[0, 0]).astype(jnp.float32)
        values = []
        for row in range(3):
            value = jnp.zeros((1, 256), jnp.float32)
            for option in range(table.shape[1]):
                value = jnp.where(kind == option, table[row, option], value)
            values.append(value)
        for row in range(3):
            sent[half, row : row + 1, :] = anchor[row, 0, :, lanes].astype(jnp.float32)
            sent[half, row + 3 : row + 4, :] = fraction[row, 0, :, lanes]
            state[half, row : row + 1, :] = velocity[row, 0, :, lanes]
            state[half, row + 3 : row + 4, :] = jnp.zeros((1, 256), jnp.float32)
        sent[half, 6:7, :] = values[0] * live
        sent[half, 7:8, :] = values[1] * values[1]
        state[half, 6:7, :] = values[2]
        state[half, 7:8, :] = live
    for plane in range(4):
        for half in range(2):
            sent[2 + 2 * plane + half] = target[plane, pl.ds(8 * half, 8), :]


def inverse_scale(place, full, scale, scaled):
    matrix = band((1.0,) * 9)
    rows = rows_inside(place, -8, 32)
    planes = [full[index // 4, pl.ds(6 + index % 4 * 4, 4)] for index in range(2, 19)]
    planes = jnp.stack([plane.reshape(32, 256) for plane in planes])
    sums = []
    for source in (planes, planes * planes):
        pairs = source[0:16] + source[1:17]
        fours = pairs[0:14] + pairs[2:16]
        summed = fours[0:9] + fours[4:13] + source[8:17]
        sums.append(depth_filtered(rows_boxed(summed), matrix, 3) * (1.0 / 729.0))
    value = lax.rsqrt(sums[1] - sums[0] * sums[0] + EPSILON)
    for plane in range(9):
        kept = jnp.where(rows, value[plane], 0.0) * plane_inside(place, plane - 2)
        scale[plane] = kept
        scaled[plane] = kept * planes[plane + 4]


def place_of(state, extent):
    return (state[2, 0:1, :], state[2, 1:2, :], *extent)


def add_pair_block(block, pair_blocks, count):
    pair_blocks[count, 0:3, :] = KAPPA * (block[0:3] + block[3:6])
    pair_blocks[count, 3:4, :] = -block[6:7]
    pair_blocks[count, 4:5, :] = block[7:8]
    return count + (block[6, 0] > 0.0).astype(jnp.int32)


def pair_sums(state, pair_blocks, pair_count, own_columns, sums_in, sums_out):
    pair_blocks[pair_count] = jnp.zeros((8, LANES), jnp.float32)
    count = state[2, 2, 0].astype(jnp.int32)

    def add_rows(index, carry):
        rows = pl.ds(index * I_ROWS, I_ROWS)
        own_x, own_y, own_z, own_s = (own_columns[row, rows, :] for row in range(4))

        def add_blocks(step, totals):
            for part in range(2):
                block = pair_blocks[step * 2 + part]
                x = own_x - block[0:1]
                y = own_y - block[1:2]
                z = own_z - block[2:3]
                spread = own_s - block[4:5]
                inverse = 1.0 / spread
                factor = jnp.exp2((x * x + y * y + z * z) * inverse)
                factor = (factor * block[3:4]) * inverse
                totals = (totals[0] + factor * x, totals[1] + factor * y, totals[2] + factor * z)
            return totals

        if sums_in is None:
            totals = (jnp.zeros((I_ROWS, LANES), jnp.float32),) * 3
        else:
            totals = tuple(sums_in[axis, rows, :] for axis in range(3))
        totals = lax.fori_loop(0, (pair_count + 1) // 2, add_blocks, totals)
        for axis in range(3):
            sums_out[axis, rows, :] = totals[axis]
        return carry

    lax.fori_loop(0, (count + I_ROWS - 1) // I_ROWS, add_rows, 0)


def chunk_density(chunk, planes, place):
    depth = iota((256, 256), 0).astype(jnp.float32)
    height = iota((32, 256), 0).astype(jnp.float32) - 8.0
    fx, fy, fz = chunk[3:4], chunk[4:5], chunk[5:6]
    charge = chunk[6:7]
    selected = jnp.where(depth == chunk[2:3], 1.0, 0.0).astype(jnp.bfloat16)
    weight_y = jnp.where(
        height == chunk[1:2], 1.0 - fy, jnp.where(height == chunk[1:2] + 1.0, fy, 0.0)
    )
    weight_y = jnp.where(rows_inside(place, -8, 32), weight_y, 0.0)
    weights = []
    for amount in (charge * (1.0 - fz), charge * fz):
        for plane in planes:
            weight_x = jnp.where(
                chunk[0:1] == plane, 1.0 - fx, jnp.where(chunk[0:1] + 1.0 == plane, fx, 0.0)
            )
            weights.append((weight_x * amount * plane_inside(place, plane)) * weight_y)
    added = dot_exact(jnp.concatenate(weights, 0), selected, ((1,), (1,)))
    return added.reshape(2, len(planes), 32, 256)


def joined(block, moved):
    return jnp.concatenate([block[0:3], moved[0:3], block[6:8]], 0)


def own_kernel(moving, extent, sent, state, *refs):
    if moving:
        fractions, own_columns, sums, spread, pair_blocks = refs
    else:
        staged, own_columns, sums, spread, pair_blocks = refs
        staged[...] = state[...]
    place = place_of(state, extent)
    pair_count = jnp.int32(0)
    spread[...] = jnp.zeros(spread.shape, jnp.float32)
    for half in range(2):
        own = joined(sent[half], fractions[half]) if moving else sent[half]
        packed = jnp.concatenate(
            [KAPPA * (own[0:3] + own[3:6]), own[7:8], jnp.zeros((4, 256), jnp.float32)], 0
        )
        turned = jnp.transpose(packed)
        rows = pl.ds(half * 256, 256)
        for row in range(3):
            own_columns[row, rows, :] = jnp.broadcast_to(turned[:, row : row + 1], (256, LANES))
        own_columns[3, rows, :] = jnp.broadcast_to(-turned[:, 3:4], (256, LANES))
        for part in range(2):
            block = own[:, part * LANES : (part + 1) * LANES]
            pair_count = add_pair_block(block, pair_blocks, pair_count)

        @pl.when(own[6, 0] > 0.0)
        def _(own=own):
            spread[...] += chunk_density(own, range(5), place)

    pair_sums(state, pair_blocks, pair_count, own_columns, None, sums)


def column_kernel(moving, full, state, *refs):
    if moving:
        fractions, own_columns, sums_in, sums, pair_blocks = refs
    else:
        own_columns, sums_in, sums, pair_blocks = refs
    pair_count = jnp.int32(0)
    row_index = iota((8, LANES), 0)
    for side in (0, 2):
        shift = jnp.where(row_index == 1, 16.0 * (side - 1), 0.0)
        for part in range(4):
            lanes = pl.ds((part % 2) * LANES, LANES)
            block = full[0, side * 2 + part // 2, :, lanes]
            if moving:
                block = joined(block, fractions[0, side, part // 2, :, lanes])
            pair_count = add_pair_block(block + shift, pair_blocks, pair_count)
    pair_sums(state, pair_blocks, pair_count, own_columns, sums_in, sums)


def step_kernel(last, extent, full, state, own_columns, sums_in, spread, *refs):
    place = place_of(state, extent)
    if last:
        fractions, scale, scaled, final_velocity, displacement, potential_out = refs[:6]
    else:
        fractions_out, state_out, scale, scaled = refs[:4]
    pair_blocks, spread_blocks, sums, density = refs[-4:]
    for part in range(2):
        density[part, 0:4] = jnp.zeros((4, 32, 256), jnp.float32)
        density[part, 4:9] = spread[part]
        density[part, 9:13] = jnp.zeros((4, 32, 256), jnp.float32)
    spread_blocks[...] = jnp.zeros(spread_blocks.shape, jnp.float32)

    def block_of(column, index, lanes):
        block = full[column, index, :, lanes]
        if last:
            return joined(block, fractions[column, index // 2, index % 2, :, lanes])
        return block

    row_index = iota((8, LANES), 0)
    pair_count = jnp.int32(0)
    spread_counts = []
    for column in range(5):
        spread_count = jnp.int32(0)
        for side in range(3):
            if (column, side) == (2, 1):
                continue
            shift = jnp.where(
                row_index == 0,
                4.0 * (column - 2),
                jnp.where(row_index == 1, 16.0 * (side - 1), 0.0),
            )
            for part in range(4):
                lanes = pl.ds((part % 2) * LANES, LANES)
                block = block_of(column, side * 2 + part // 2, lanes) + shift
                spread_blocks[column, spread_count] = block
                spread_count = spread_count + (block[6, 0] > 0.0).astype(jnp.int32)
                if column in (1, 3):
                    pair_count = add_pair_block(block, pair_blocks, pair_count)
        spread_counts.append(spread_count)
    pair_sums(state, pair_blocks, pair_count, own_columns, sums_in, sums)

    def add_chunks(step, carry):
        added = []
        for column, planes in enumerate(
            ((-4,), range(-4, 1), range(0, 5), range(4, 9), (8,))
        ):
            chunk = jnp.concatenate(
                [spread_blocks[column, step * 2], spread_blocks[column, step * 2 + 1]], 1
            )
            added.append(chunk_density(chunk, planes, place))
        for part in range(2):
            far_left, left, own, right, far_right = (added[column][part] for column in range(5))
            pieces = (
                far_left + left[0:1],
                left[1:4],
                left[4:5] + own[0:1],
                own[1:4],
                own[4:5] + right[0:1],
                right[1:4],
                right[4:5] + far_right,
            )
            start = 0
            for piece in pieces:
                where = pl.ds(start, piece.shape[0])
                density[part, where] = density[part, where] + piece
                start += piece.shape[0]
        return carry

    longest = functools.reduce(jnp.maximum, spread_counts)
    lax.fori_loop(0, (longest + 1) // 2, add_chunks, 0)

    if not last:
        inverse_scale(place, full, scale, scaled)
    matrix = band(BLUR)
    value = density[0] + pltpu.roll(density[1], 1, 2)
    value = depth_filtered(rows_blurred(planes_blurred(value, 9)), matrix, 2)
    residual = value * scale[...] - scaled[...]
    potential = depth_filtered(rows_blurred(planes_blurred(residual, 5)), matrix, 2)
    if last:
        potential_out[...] = potential[0:4, 8:24]

    field = potential[:, 8:32].reshape(120, 256)
    both = jnp.concatenate([field, pltpu.roll(field, 255, 1)], 0)
    ones = jnp.ones((8, LANES), jnp.bfloat16)
    depth = iota((256, 256), 0).astype(jnp.float32)
    height = iota((24, 256), 0).astype(jnp.float32)
    rows = rows_inside(place, 0, 24)
    edge = plane_inside(place, 4)
    for half in range(2):
        own = jnp.concatenate([block_of(2, 2 + half, pl.ds(i * LANES, LANES)) for i in range(2)], 1)
        gx, gy, gz, fx, fy, fz = (own[row : row + 1] for row in range(6))
        selected = jnp.where(depth == gz, 1.0, 0.0).astype(jnp.bfloat16)
        taken = dot_exact(both, selected, ((1,), (0,))).reshape(2, 5, 24, 256)
        lower, upper = (height == gy) & rows, (height == gy + 1.0) & rows
        weight_y = jnp.where(lower, 1.0 - fy, jnp.where(upper, fy, 0.0))
        slope_y = jnp.where(lower, -1.0, jnp.where(upper, 1.0, 0.0))
        mixed = [jnp.zeros((24, 256), jnp.float32) for _ in range(3)]
        for plane in range(5):
            slope_z = taken[1, plane] - taken[0, plane]
            product = taken[0, plane] + fz * slope_z
            lower, upper = gx == plane, gx + 1.0 == plane
            weight_x = jnp.where(lower, 1.0 - fx, jnp.where(upper, fx, 0.0))
            slope_x = jnp.where(lower, -1.0, jnp.where(upper, 1.0, 0.0))
            if plane == 4:
                weight_x, slope_x = weight_x * edge, slope_x * edge
            mixed[0] = mixed[0] + slope_x * product
            mixed[1] = mixed[1] + weight_x * product
            mixed[2] = mixed[2] + weight_x * slope_z
        gradient = (
            jnp.sum(mixed[0] * weight_y, 0, keepdims=True),
            jnp.sum(mixed[1] * slope_y, 0, keepdims=True),
            jnp.sum(mixed[2] * weight_y, 0, keepdims=True),
        )
        charge = own[6:7]
        values = state[half]
        mass, live = values[6:7], values[7:8]
        if not last:
            state_out[half, 6:8, :] = values[6:8]
            state_out[2] = state[2]
            fractions_out[half, 3:4, :] = jnp.zeros((1, 256), jnp.float32)
        for axis in range(3):
            parts = split(sums[axis, pl.ds(half * 256, 256), :], 2)
            pair = dot(ones, parts[0], ((1,), (1,))) + dot(ones, parts[1], ((1,), (1,)))
            force = charge * (pair[0:1] * (1.0 / KAPPA) - gradient[axis])
            force = jnp.where(charge > 0.0, force, 0.0)
            velocity = values[axis : axis + 1] + TIME_STEP * force / mass
            moved = values[axis + 3 : axis + 4] + TIME_STEP * velocity
            if last:
                lanes = pl.ds(half * 256, 256)
                final_velocity[axis, 0, :, lanes] = velocity * live
                displacement[axis, 0, :, lanes] = moved * live
            else:
                state_out[half, axis : axis + 1, :] = velocity
                state_out[half, axis + 3 : axis + 4, :] = moved
                fractions_out[half, axis : axis + 1, :] = (
                    own[axis + 3 : axis + 4] + TIME_STEP * velocity
                )


SMEM = pl.BlockSpec(memory_space=pltpu.SMEM)
VMEM = pl.BlockSpec(memory_space=pltpu.VMEM)


def shape(*dims):
    return jax.ShapeDtypeStruct(dims, jnp.float32)


def links():
    chips = lax.axis_size("cells") // 2
    groups = lax.axis_size("grp")

    def coloured(count, first):
        pairs = []
        for left in range(first, count - 1, 2):
            pairs += [(left, left + 1), (left + 1, left)]
        return pairs

    def doubled(pairs):
        return [(2 * a + core, 2 * b + core) for a, b in pairs for core in range(2)]

    return {
        "odd": ("cells", doubled(coloured(chips, 1))),
        "even": ("cells", doubled(coloured(chips, 0))),
        "rows_even": ("grp", coloured(groups, 0)),
        "rows_odd": ("grp", coloured(groups, 1)),
        "pair": ("cells", [(i, i ^ 1) for i in range(2 * chips)]),
    }


def spread_out(own, rows, groups, flags):
    even_chip, even_row, _ = flags

    def send(value, link):
        return lax.ppermute(value, *groups[link])

    odd = send(own, "odd")
    even = send(own, "even")
    left = jnp.where(even_chip, odd, even)
    right = jnp.where(even_chip, even, odd)
    columns = jnp.stack([own, left, right])
    from_even = send(rows(columns, even_row), "rows_even")
    from_odd = send(rows(columns, ~even_row), "rows_odd")
    above = jnp.where(even_row, from_even, from_odd)
    below = jnp.where(even_row, from_odd, from_even)

    def send_partner(value):
        return send(value, "pair")

    return columns, below, above, send_partner


def finish(full, send, first_core):
    chosen = jnp.where(first_core, full[2], full[1])
    got = send(jnp.stack([full[0], chosen]))
    minus = jnp.where(first_core, got[1], got[0])
    plus = jnp.where(first_core, got[0], got[1])
    return jnp.stack([full[1], minus, full[0], plus, full[2]])


def per_device(fraction, velocity, anchor, atom_types, counts, type_table, target):
    cells, groups_count = lax.axis_size("cells"), lax.axis_size("grp")
    cell, group = lax.axis_index("cells"), lax.axis_index("grp")
    groups = links()
    flags = ((cell // 2) % 2 == 0, group % 2 == 0, cell % 2 == 0)
    extent = (4.0 * cells, 16.0 * groups_count)

    raw = [
        pltpu.with_memory_space_constraint(value, pltpu.HBM)
        for value in (type_table, fraction, velocity, anchor, atom_types, target)
    ]
    own, state = pl.pallas_call(
        prep_kernel,
        out_shape=(shape(10, 8, 256), shape(3, 8, 256)),
        in_specs=[SMEM] + [pl.BlockSpec(memory_space=pltpu.HBM)] * 6,
        out_specs=(VMEM, VMEM),
        scratch_shapes=[pltpu.SMEM(type_table.shape, jnp.float32)]
        + [pltpu.VMEM(value.shape, value.dtype) for value in raw[1:]]
        + [pltpu.SemaphoreType.DMA((6,))],
        name="prep",
        compiler_params=pltpu.CompilerParams(vmem_limit_bytes=24 << 20),
    )(counts, *raw)

    table = shape(4, 512, LANES)
    totals = shape(3, 512, LANES)
    spread = shape(2, 5, 32, 256)
    limit = pltpu.CompilerParams(vmem_limit_bytes=24 << 20)

    def alone(turn, *operands):
        outs = (table, totals, spread)
        if turn == 0:
            outs = (shape(3, 8, 256),) + outs
        return pl.pallas_call(
            functools.partial(own_kernel, turn > 0, extent),
            out_shape=outs,
            in_specs=[VMEM] * len(operands),
            out_specs=(VMEM,) * len(outs),
            scratch_shapes=[pltpu.VMEM((6, 8, LANES), jnp.float32)],
            name="alone",
            compiler_params=limit,
        )(*operands)

    def beside(turn, *operands):
        return pl.pallas_call(
            functools.partial(column_kernel, turn > 0),
            out_shape=totals,
            in_specs=[VMEM] * len(operands),
            out_specs=VMEM,
            scratch_shapes=[pltpu.VMEM((10, 8, LANES), jnp.float32)],
            name="beside",
            compiler_params=limit,
        )(*operands)

    state, own_columns, sums, own_spread = alone(0, own, state)

    def rows_first(columns, upper):
        fields = columns[:, 2:].reshape(3, 4, 2, 8, 256)
        return jnp.concatenate(
            [columns[:, :2], jnp.where(upper, fields[:, :, 1], fields[:, :, 0])], 1
        )

    columns, below, above, send = spread_out(own, rows_first, groups, flags)
    full = jnp.concatenate(
        [
            jnp.stack([below[:, :2], columns[:, :2], above[:, :2]], 1).reshape(3, 6, 8, 256),
            jnp.concatenate(
                [
                    below[:, 2:, None],
                    columns[:, 2:].reshape(3, 4, 2, 8, 256),
                    above[:, 2:, None],
                ],
                2,
            ).reshape(3, 16, 8, 256),
        ],
        1,
    )
    column = full
    sums = beside(0, column, state, own_columns, sums)
    full = finish(full, send, flags[2])

    field = shape(9, 32, 256)
    scratch = [
        pltpu.VMEM((26, 8, LANES), jnp.float32),
        pltpu.VMEM((5, 14, 8, LANES), jnp.float32),
        pltpu.VMEM((3, 512, LANES), jnp.float32),
        pltpu.VMEM((2, 13, 32, 256), jnp.float32),
    ]
    fractions, state, scale, scaled = pl.pallas_call(
        functools.partial(step_kernel, False, extent),
        out_shape=(shape(2, 4, 256), shape(3, 8, 256), field, field),
        in_specs=[VMEM] * 5,
        out_specs=(VMEM,) * 4,
        scratch_shapes=scratch,
        name="step",
        compiler_params=pltpu.CompilerParams(vmem_limit_bytes=24 << 20),
    )(full, state, own_columns, sums, own_spread)

    own_columns, sums, own_spread = alone(1, own, state, fractions)

    columns, below, above, send = spread_out(fractions, lambda c, upper: c, groups, flags)
    moved = jnp.stack([below, columns, above], 1)
    sums = beside(1, column, state, moved, own_columns, sums)
    moved = finish(moved, send, flags[2])
    return pl.pallas_call(
        functools.partial(step_kernel, True, extent),
        out_shape=(shape(*velocity.shape), shape(*velocity.shape), shape(*target.shape)),
        in_specs=[VMEM] * 8,
        out_specs=(VMEM,) * 3,
        scratch_shapes=scratch,
        name="step_last",
        compiler_params=pltpu.CompilerParams(vmem_limit_bytes=24 << 20),
    )(full, state, own_columns, sums, own_spread, moved, scale, scaled)


def solution(mesh):
    placed = (
        P(None, "cells", "grp", None),
        P(None, "cells", "grp", None),
        P(None, "cells", "grp", None),
        P("cells", "grp", None),
        P("cells", "grp"),
        P(),
        P("cells", "grp", None),
    )
    return jax.shard_map(
        per_device,
        mesh=mesh,
        in_specs=placed,
        out_specs=(
            P(None, "cells", "grp", None),
            P(None, "cells", "grp", None),
            P("cells", "grp", None),
        ),
        check_vma=False,
    )
```
